128 devices in a mesh: tm: 4 (over x), grid: 32 (over y, z, core).
Axes of the slice: x: 4, y: 4, z: 4, core: 2. Of those that a mesh axis runs over, the one named last changes fastest.
Arguments:
- clocked_seawarmth: bfloat16 [4096, 98304], P(('tm', 'grid')), may hold values from -12 to 12
- clocked_precipitation: bfloat16 [4096, 98304], P(('tm', 'grid')), may hold values from -12 to 12
- fading_weights: float32 [2, 4096], P(None, 'tm'), may hold values from 0.4 to 1, as said below
- starting_average: float32 [2, 98304], P(None, 'grid'), may hold values from -6 to 6
- warmth_random_operator: bfloat16 [98304, 256], P('grid'), may hold values from -0.01953125 to 0.01953125
- wetness_random_operator: bfloat16 [98304, 256], P('grid'), may hold values from -0.01953125 to 0.01953125
Outputs:
- warmth_summary: float32 [256, 98304], P('tm', 'grid')
- wetness_summary: float32 [256, 98304], P('tm', 'grid')
- kernel_middle: float32 [256, 256], replicated
The draws below stay inside these ranges and needn't reach their ends.
Inputs may be any that keep to these rules, and one draw needn't show every extreme that they name: `fading_weights`: each factor lies below one.
All inputs are finite; a program needn't handle non-finite values.
Results may differ from the reference program's by a relative error of at most 0.0085.
Values may be sent and summed in bfloat16 or wider, within the bound.
No kernel may reach another device: no remote copies, remote signals or barrier semaphores. Data moves between devices by JAX's collectives and lax.ppermute only.
A program may use at most 192 MiB of HBM per device.

```python
import jax
import jax.numpy as jnp
from jax import lax

PROBE_COUNT = 256
SPAN_CLOCKTIMES = 4096
MESH_SITES = 98304


def draw_field(key):
    key_scale, key_values = jax.random.split(key, 2)
    point_scale = jnp.exp(jax.random.uniform(key_scale, (1, MESH_SITES), jnp.float32, jnp.log(0.3), jnp.log(3.0)))
    quantity_lines = jnp.clip(jax.random.normal(key_values, (SPAN_CLOCKTIMES, MESH_SITES), jnp.float32), -4.0, 4.0)
    return jnp.clip(quantity_lines * point_scale, -12.0, 12.0)


def draw_clocked_seawarmth(key, part):
    return draw_field(jax.random.fold_in(key, 101)).astype(jnp.bfloat16)


def draw_clocked_precipitation(key, part):
    return draw_field(jax.random.fold_in(key, 202)).astype(jnp.bfloat16)


def draw_fading_weights(key, part):
    divide_seeds = jax.random.split(jax.random.fold_in(key, 303), 6)
    slow_rate = jnp.exp(jax.random.uniform(divide_seeds[0], (2,), jnp.float32, jnp.log(0.0001), jnp.log(0.0003)))
    fast_rate = jnp.exp(jax.random.uniform(divide_seeds[1], (2,), jnp.float32, jnp.log(0.02), jnp.log(0.035)))
    chosen = jax.random.randint(divide_seeds[2], (), 0, 2)
    base_rate = jnp.where(jnp.arange(2) == chosen, fast_rate, slow_rate)
    roughness = jnp.exp(jax.random.uniform(divide_seeds[3], (2, SPAN_CLOCKTIMES), jnp.float32, jnp.log(0.5), jnp.log(2.0)))
    fading_multiplier = 1.0 - base_rate[:, None] * roughness
    spike_location = jax.random.randint(divide_seeds[4], (3,), 0, SPAN_CLOCKTIMES)
    spike_segment = jnp.any(jnp.arange(SPAN_CLOCKTIMES)[None, :] == spike_location[:, None], axis=0)
    spike_cutoff = jax.random.uniform(divide_seeds[5], (2, SPAN_CLOCKTIMES), jnp.float32, 0.5, 0.8)
    return jnp.where(spike_segment[None, :], fading_multiplier * spike_cutoff, fading_multiplier)


def block_levels(stream_key, shape, cuts, low, high):
    def one(dim, shards_of):
        heights = jax.random.uniform(jax.random.fold_in(jax.random.fold_in(stream_key, 6), dim), (shards_of,), jnp.float32, low / len(cuts), high / len(cuts))
        return jnp.repeat(jnp.exp(heights), shape[dim] // shards_of).reshape((-1,) + (1,) * (len(shape) - dim - 1))

    level = one(*cuts[0])
    for cut in cuts[1:]:
        level = level * one(*cut)
    return level


def noise(key, shape, spread, bound, cuts=(), held_as=jnp.bfloat16):
    array = spread * jax.random.normal(key, shape, jnp.float32)
    if cuts:
        array = array * block_levels(key, shape, cuts, -0.22, 0.18)
    return jnp.clip(array, -bound, bound).astype(held_as)


def setup_inputs(seed: int = 0) -> dict:
    arg_keys = jax.random.split(jax.random.key(seed), 7)
    return {
        "clocked_seawarmth": draw_clocked_seawarmth(jax.random.fold_in(arg_keys[6], 71), 0),
        "clocked_precipitation": draw_clocked_precipitation(jax.random.fold_in(arg_keys[6], 71), 0),
        "fading_weights": draw_fading_weights(jax.random.fold_in(arg_keys[6], 71), 0),
        "starting_average": noise(arg_keys[3], (2, MESH_SITES), 1.0, 6.0, ((1, 32),), jnp.float32),
        "warmth_random_operator": noise(arg_keys[4], (MESH_SITES, PROBE_COUNT), MESH_SITES ** -0.5, 0.01953125, ((0, 32),)),
        "wetness_random_operator": noise(arg_keys[5], (MESH_SITES, PROBE_COUNT), MESH_SITES ** -0.5, 0.01953125, ((0, 32),)),
    }


def reference(clocked_seawarmth, clocked_precipitation, fading_weights, starting_average, warmth_random_operator, wetness_random_operator):
    def march_once(running, single_tick_feed):
        warmth_line, wetness_line, fading_multiplier = single_tick_feed
        quantity_lines = jnp.stack([warmth_line, wetness_line]).astype(jnp.float32)
        departure_amount = (quantity_lines - running).astype(jnp.bfloat16)
        running = fading_multiplier[:, None] * running + (1.0 - fading_multiplier[:, None]) * quantity_lines
        return running, (departure_amount[0], departure_amount[1])

    final_running_average, departure_lines = lax.scan(march_once, starting_average.astype(jnp.float32), (clocked_seawarmth, clocked_precipitation, jnp.transpose(fading_weights)))
    warmth_departure, wetness_departure = departure_lines
    warmth_compressed = jnp.dot(warmth_departure, warmth_random_operator, preferred_element_type=jnp.float32).astype(jnp.bfloat16)
    wetness_compressed = jnp.dot(wetness_departure, wetness_random_operator, preferred_element_type=jnp.float32).astype(jnp.bfloat16)
    divisor_magnitude = SPAN_CLOCKTIMES ** -0.5
    warmth_summary = jnp.dot(jnp.transpose(wetness_compressed), warmth_departure, preferred_element_type=jnp.float32) * divisor_magnitude
    wetness_summary = jnp.dot(jnp.transpose(warmth_compressed), wetness_departure, preferred_element_type=jnp.float32) * divisor_magnitude
    kernel_middle = jnp.dot(jnp.transpose(warmth_compressed), wetness_compressed, preferred_element_type=jnp.float32) * divisor_magnitude
    return warmth_summary, wetness_summary, kernel_middle
```

```python
import jax
import jax.numpy as jnp
from jax import lax
from jax.experimental import pallas as pl
from jax.experimental.pallas import tpu as pltpu
from jax.sharding import PartitionSpec as P

BLK = 256
NCHUNK = 512
Y, Z, C = 4, 4, 2
F32, BF16 = jnp.float32, jnp.bfloat16
HIGHEST = lax.Precision.HIGHEST


def decay_blocks(fading):
    nb = fading.shape[1] // BLK
    a = fading.reshape(2, nb, BLK)
    log_a = jnp.log(a)
    inclusive = jnp.cumsum(log_a, axis=2)
    before = jnp.concatenate([jnp.zeros((2, nb, 1), F32), inclusive, jnp.zeros((2, nb, 7), F32)], axis=2)
    rows, cols = BLK + 8, BLK + 128
    r = lax.broadcasted_iota(jnp.int32, (rows, cols), 0)
    c = lax.broadcasted_iota(jnp.int32, (rows, cols), 1)
    pad = lambda v: jnp.pad(v, ((0, 0), (0, 0), (0, 128)))
    spread = before[..., :, None] - pad(inclusive)[..., None, :]
    gain = pad(1.0 - a)[..., None, :]
    gain = jnp.where(c == BLK, 1.0, gain)
    weight = jnp.exp(jnp.minimum(spread, 0.0)) * gain
    weight = jnp.where((c < jnp.minimum(r, BLK)) | (c == BLK), weight, 0.0)
    sign = jnp.where((r < BLK) == (c < BLK), -1.0, 1.0)
    block = jnp.where(r == c, jnp.where(r < BLK, 1.0, sign * weight), sign * weight)
    block = jnp.where(r <= BLK, block, 0.0)
    total = inclusive[..., -1]
    ahead = jnp.cumsum(total, axis=1) - total
    since_start = jnp.exp(ahead[..., None] + before[..., :BLK]).reshape(2, nb * BLK)
    behind = jnp.cumsum(total[:, ::-1], axis=1)[:, ::-1] - total
    to_end = jnp.exp(behind[..., None] + inclusive[..., -1:] - inclusive) * (1.0 - a)
    return block, since_start, to_end.reshape(2, nb * BLK), jnp.exp(total.sum(axis=1))


def forward_kernel(x_ref, op_ref, block_ref, p_ref, end_ref, state):
    b = pl.program_id(0)

    @pl.when(b == 0)
    def _():
        state[...] = jnp.zeros_like(state)

    y = jnp.dot(x_ref[...], op_ref[...], preferred_element_type=F32)
    out = jnp.dot(block_ref[0, :, :BLK], y, precision=HIGHEST, preferred_element_type=F32)
    out = out - block_ref[0, :, BLK : BLK + 1] * state[0:1, :]
    p_ref[...] = out[:BLK]
    state[...] = out[BLK:]
    end_ref[...] = out[BLK:]


def forward(x, operator, block):
    hours, width = x.shape
    rank = operator.shape[1]
    nb = hours // BLK
    return pl.pallas_call(
        forward_kernel,
        grid=(nb,),
        in_specs=[
            pl.BlockSpec((BLK, width), lambda b: (b, 0)),
            pl.BlockSpec((width, rank), lambda b: (0, 0)),
            pl.BlockSpec((1, BLK + 8, BLK + 128), lambda b: (b, 0, 0)),
        ],
        out_specs=[
            pl.BlockSpec((BLK, rank), lambda b: (b, 0)),
            pl.BlockSpec((8, rank), lambda b: (0, 0)),
        ],
        out_shape=[
            jax.ShapeDtypeStruct((hours, rank), F32),
            jax.ShapeDtypeStruct((8, rank), F32),
        ],
        scratch_shapes=[pltpu.VMEM((8, rank), F32)],
        compiler_params=pltpu.CompilerParams(vmem_limit_bytes=24 << 20),
        cost_estimate=pl.CostEstimate(
            flops=2 * hours * width * rank, bytes_accessed=2 * hours * width, transcendentals=0
        ),
        name="forward",
    )(x, operator, block)


def backward_kernel(q_ref, block_ref, x_ref, enter_ref, w_ref, z_high, z_low, carried):
    @pl.when(pl.program_id(0) == 0)
    def _():
        nb = block_ref.shape[0]
        reverse = jnp.zeros((q_ref.shape[1], 1), F32)
        for b in reversed(range(nb)):
            q = q_ref[b * BLK : (b + 1) * BLK, :].astype(F32)
            out = jnp.dot(q.T, block_ref[b, :BLK, :], precision=HIGHEST, preferred_element_type=F32)
            out = out - reverse * block_ref[b, BLK : BLK + 1, :]
            z = out[:, :BLK]
            high = z.astype(BF16)
            z_high[:, b * BLK : (b + 1) * BLK] = high
            z_low[:, b * BLK : (b + 1) * BLK] = (z - high.astype(F32)).astype(BF16)
            reverse = out[:, BLK : BLK + 1]
        carried[...] = jnp.broadcast_to(reverse, carried.shape)

    x = x_ref[...]
    w = jnp.dot(z_high[...], x, preferred_element_type=F32)
    w = w + jnp.dot(z_low[...], x, preferred_element_type=F32)
    w = w - carried[:, 0:1] * enter_ref[0:1, :]
    w_ref[...] = w.astype(w_ref.dtype)


def backward(q, block, x, enter):
    hours, width = x.shape
    rank = q.shape[1]
    nb = hours // BLK
    return pl.pallas_call(
        backward_kernel,
        grid=(width // NCHUNK,),
        in_specs=[
            pl.BlockSpec((hours, rank), lambda n: (0, 0)),
            pl.BlockSpec((nb, BLK + 8, BLK + 128), lambda n: (0, 0, 0)),
            pl.BlockSpec((hours, NCHUNK), lambda n: (0, n)),
            pl.BlockSpec((8, NCHUNK), lambda n: (0, n)),
        ],
        out_specs=pl.BlockSpec((rank, NCHUNK), lambda n: (0, n)),
        out_shape=jax.ShapeDtypeStruct((rank, width), BF16),
        scratch_shapes=[
            pltpu.VMEM((rank, hours), BF16),
            pltpu.VMEM((rank, hours), BF16),
            pltpu.VMEM((rank, 128), F32),
        ],
        compiler_params=pltpu.CompilerParams(vmem_limit_bytes=24 << 20),
        cost_estimate=pl.CostEstimate(
            flops=4 * hours * width * rank, bytes_accessed=2 * hours * width, transcendentals=0
        ),
        name="backward",
    )(q, block, x, enter)


def middle_kernel(left_ref, right_ref, out_ref):
    out = jnp.dot(left_ref[...].astype(F32).T.astype(BF16), right_ref[...], preferred_element_type=F32)
    out_ref[...] = out.astype(out_ref.dtype)


def cross(left, right):
    rank = left.shape[1]
    return pl.pallas_call(
        middle_kernel,
        out_shape=jax.ShapeDtypeStruct((rank, rank), BF16),
        in_specs=[pl.BlockSpec(memory_space=pltpu.VMEM)] * 2,
        out_specs=pl.BlockSpec(memory_space=pltpu.VMEM),
        compiler_params=pltpu.CompilerParams(vmem_limit_bytes=8 << 20),
        cost_estimate=pl.CostEstimate(flops=2 * left.size * rank, bytes_accessed=4 * left.size, transcendentals=0),
        name="cross",
    )(left, right)


def all_to_all(x, axis, groups=None):
    return lax.all_to_all(x, axis, split_axis=0, concat_axis=0, tiled=True, axis_index_groups=groups)


def pick(x, i):
    return lax.dynamic_index_in_dim(x, i, 0, keepdims=False)


def shifted(x, by):
    n = lax.axis_size("tm")
    return lax.ppermute(x, "tm", [(i, (i + by) % n) for i in range(n)])


def entering(end, gain, start):
    message = jnp.concatenate([end[None], jnp.broadcast_to(gain, (1, end.shape[0])), jnp.zeros((6, end.shape[0]), F32)])
    i = lax.axis_index("tm")
    total, so_far = jnp.zeros_like(end), jnp.ones_like(end)
    for d in range(1, lax.axis_size("tm")):
        got = shifted(message, d)
        total = total + jnp.where(i >= d, so_far * got[0], 0.0)
        so_far = so_far * jnp.where(i >= d, got[1], 1.0)
    return total + so_far * start


def grid_place():
    g = lax.axis_index("grid")
    return g // (Z * C), (g // C) % Z, g % C


def along(x, dim, by):
    def moved(g):
        y, z, c = g // (Z * C), (g // C) % Z, g % C
        y, z, c = ((y + by) % Y, z, c) if dim == "y" else (y, (z + by) % Z, c) if dim == "z" else (y, z, 1 - c)
        return (y * Z + z) * C + c

    return lax.ppermute(x, "grid", [(g, moved(g)) for g in range(Y * Z * C)])


def scattered(x, dim, me, n):
    out = pick(x, me)
    for by in range(1, n):
        out = out + along(pick(x, (me + by) % n), dim, by)
    return out


def gathered(x, dim, me, n):
    out = jnp.zeros((n, *x.shape), x.dtype)
    out = lax.dynamic_update_index_in_dim(out, x, me, 0)
    for by in range(1, n):
        out = lax.dynamic_update_index_in_dim(out, along(x, dim, by), (me + n - by) % n, 0)
    return out


def summed_by_permutes(p):
    y, z, c = grid_place()
    hours, rank = p.shape
    rows = hours // (Y * Z * C)
    p = scattered(p.reshape(C, Y * Z * rows, rank), "core", c, C)
    p = scattered(p.reshape(Y, Z * rows, rank), "y", y, Y)
    p = scattered(p.reshape(Z, rows, rank), "z", z, Z)
    q = gathered(p.astype(BF16), "z", z, Z).reshape(Z * rows, rank)
    q = gathered(q, "y", y, Y).reshape(Y * Z * rows, rank)
    return gathered(q, "core", c, C).reshape(hours, rank)


def summed_by_all_to_all(p, *held):
    _, _, c = grid_place()
    hours, rank = p.shape
    n = Y * Z
    rows = hours // (n * C)
    groups = [[k * C + core for k in range(n)] for core in range(C)]
    p = scattered(p.reshape(C, n * rows, rank), "core", c, C).astype(BF16)
    p, *held = lax.optimization_barrier((p, *held))
    p = all_to_all(p.reshape(n, rows, rank), "grid", groups)
    q = p.astype(F32).sum(axis=0).astype(BF16)
    q = all_to_all(jnp.broadcast_to(q, (n, rows, rank)), "grid", groups)
    q = gathered(q.reshape(n * rows, rank), "core", c, C).reshape(hours, rank)
    return q, *held


def summed_over_hours(w):
    n = lax.axis_size("tm")
    rank, width = w.shape
    w = w.reshape(n, rank // n, width)
    i, half = lax.axis_index("tm"), width // 2
    own, ahead, far, back = (pick(w, (i + k) % n) for k in range(n))
    add = lambda a, b: a.astype(F32) + b.astype(F32)
    up = shifted(far[:, :half], 1)
    down = shifted(far[:, half:], n - 1)
    from_below = shifted(ahead[:, half:], 1)
    from_above = shifted(back[:, :half], n - 1)
    up = shifted(add(up, ahead[:, :half]).astype(BF16), 1)
    down = shifted(add(down, back[:, half:]).astype(BF16), n - 1)
    left = add(own[:, :half], from_above) + up.astype(F32)
    right = add(own[:, half:], from_below) + down.astype(F32)
    return jnp.concatenate([left, right], axis=1)


def per_device(x0, x1, fading, starting, operator0, operator1):
    grid = lax.axis_size("grid")
    rows, points = x0.shape
    width, hours = points // grid, rows * grid
    scale = (hours * lax.axis_size("tm")) ** -0.5

    def tile(x):
        x = x.reshape(rows, grid, width).transpose(1, 0, 2)
        return all_to_all(x, "grid").reshape(hours, width)

    block, since_start, to_end, gain = decay_blocks(fading)
    operators = (operator0, operator1)

    def start_projection(f):
        s = starting[f]
        parts = []
        for _ in range(3):
            part = s.astype(BF16)
            parts.append(part)
            s = s - part.astype(F32)
        return jnp.dot(jnp.stack(parts), operators[f], preferred_element_type=F32).sum(axis=0)

    def partial_projection(f, x):
        p, end = forward(x, operators[f], block[f])
        enter = entering(end[0], gain[f], start_projection(f))
        return p - since_start[f][:, None] * enter[None]

    def entering_mean(f, x):
        end = (x.astype(F32) * to_end[f][:, None]).sum(axis=0)
        enter = entering(end, gain[f], starting[f])
        return jnp.broadcast_to(enter[None], (8, width))

    t0 = tile(x0)
    t1 = tile(x1)
    p0 = partial_projection(0, t0)
    q0 = summed_by_permutes(p0)
    mean0 = entering_mean(0, t0)
    t1, q0, mean0 = lax.optimization_barrier((t1, q0, mean0))
    p1 = partial_projection(1, t1)
    q1, t1 = summed_by_all_to_all(p1, t1)
    mean1 = entering_mean(1, t1)
    w1 = backward(q0, block[1], t1, mean1)
    wetness = summed_over_hours(w1) * scale
    sent = cross(q0, q1)
    middle = sent.astype(F32)
    for d in range(1, lax.axis_size("tm")):
        middle = middle + shifted(sent, d).astype(F32)
    w0 = backward(q1, block[0], t0, mean0)
    warmth = summed_over_hours(w0) * scale
    return warmth, wetness, middle * scale


def solution(mesh):
    return jax.shard_map(
        per_device,
        mesh=mesh,
        in_specs=(
            P(("tm", "grid"), None),
            P(("tm", "grid"), None),
            P(None, "tm"),
            P(None, "grid"),
            P("grid", None),
            P("grid", None),
        ),
        out_specs=(P("tm", "grid"), P("tm", "grid"), P()),
        check_vma=False,
    )
```

```python
import jax
import jax.numpy as jnp
from jax import lax
from jax.experimental import pallas as pl
from jax.experimental.pallas import tpu as pltpu
from jax.sharding import PartitionSpec as P


BLK = 256
NCHUNK = 512
Y, Z, C = 4, 4, 2
F32, BF16 = jnp.float32, jnp.bfloat16
HIGHEST = lax.Precision.HIGHEST


def decay_blocks(fading):
    nb = fading.shape[1] // BLK
    a = fading.reshape(2, nb, BLK)
    log_a = jnp.log(a)
    inclusive = jnp.cumsum(log_a, axis=2)
    before = jnp.concatenate([jnp.zeros((2, nb, 1), F32), inclusive, jnp.zeros((2, nb, 7), F32)], axis=2)
    rows, cols = BLK + 8, BLK + 128
    r = lax.broadcasted_iota(jnp.int32, (rows, cols), 0)
    c = lax.broadcasted_iota(jnp.int32, (rows, cols), 1)
    pad = lambda v: jnp.pad(v, ((0, 0), (0, 0), (0, 128)))
    spread = before[..., :, None] - pad(inclusive)[..., None, :]
    gain = pad(1.0 - a)[..., None, :]
    gain = jnp.where(c == BLK, 1.0, gain)
    weight = jnp.exp(jnp.minimum(spread, 0.0)) * gain
    weight = jnp.where((c < jnp.minimum(r, BLK)) | (c == BLK), weight, 0.0)
    sign = jnp.where((r < BLK) == (c < BLK), -1.0, 1.0)
    block = jnp.where(r == c, jnp.where(r < BLK, 1.0, sign * weight), sign * weight)
    block = jnp.where(r <= BLK, block, 0.0)
    total = inclusive[..., -1]
    ahead = jnp.cumsum(total, axis=1) - total
    since_start = jnp.exp(ahead[..., None] + before[..., :BLK]).reshape(2, nb * BLK)
    behind = jnp.cumsum(total[:, ::-1], axis=1)[:, ::-1] - total
    to_end = jnp.exp(behind[..., None] + inclusive[..., -1:] - inclusive) * (1.0 - a)
    return block, since_start, to_end.reshape(2, nb * BLK), jnp.exp(total.sum(axis=1))


def pack_kernel(x0_ref, x1_ref, out_ref):
    out_ref[0, 0] = x0_ref[...]
    out_ref[0, 1] = x1_ref[...]


def pack(x0, x1, n):
    rows, points = x0.shape
    width = points // n
    return pl.pallas_call(
        pack_kernel,
        grid=(n,),
        in_specs=[pl.BlockSpec((rows, width), lambda i: (0, i))] * 2,
        out_specs=pl.BlockSpec((1, 2, rows, width), lambda i: (i, 0, 0, 0)),
        out_shape=jax.ShapeDtypeStruct((n, 2, rows, width), x0.dtype),
        compiler_params=pltpu.CompilerParams(vmem_limit_bytes=16 << 20),
        cost_estimate=pl.CostEstimate(flops=0, bytes_accessed=8 * x0.size, transcendentals=0),
        name="pack",
    )(x0, x1)


def forward_kernel(x_ref, op_ref, block_ref, p_ref, end_ref, state):
    b = pl.program_id(1)

    @pl.when(b == 0)
    def _():
        state[...] = jnp.zeros_like(state)

    x = x_ref[:, 0].reshape(BLK, x_ref.shape[3])
    y = jnp.dot(x, op_ref[0], preferred_element_type=F32)
    out = jnp.dot(block_ref[0, 0, :, :BLK], y, precision=HIGHEST, preferred_element_type=F32)
    out = out - block_ref[0, 0, :, BLK : BLK + 1] * state[0:1, :]
    p_ref[0] = out[:BLK]
    state[...] = out[BLK:]
    end_ref[0] = out[BLK:]


def forward(x, operators, block):
    n, _, rows, width = x.shape
    rank = operators.shape[2]
    hours = n * rows
    nb, per = hours // BLK, BLK // rows
    return pl.pallas_call(
        forward_kernel,
        grid=(2, nb),
        in_specs=[
            pl.BlockSpec((per, 1, rows, width), lambda f, b: (b, f, 0, 0)),
            pl.BlockSpec((1, width, rank), lambda f, b: (f, 0, 0)),
            pl.BlockSpec((1, 1, BLK + 8, BLK + 128), lambda f, b: (f, b, 0, 0)),
        ],
        out_specs=[
            pl.BlockSpec((1, BLK, rank), lambda f, b: (f, b, 0)),
            pl.BlockSpec((1, 8, rank), lambda f, b: (f, 0, 0)),
        ],
        out_shape=[
            jax.ShapeDtypeStruct((2, hours, rank), F32),
            jax.ShapeDtypeStruct((2, 8, rank), F32),
        ],
        scratch_shapes=[pltpu.VMEM((8, rank), F32)],
        compiler_params=pltpu.CompilerParams(vmem_limit_bytes=24 << 20),
        cost_estimate=pl.CostEstimate(
            flops=4 * hours * width * rank, bytes_accessed=4 * hours * width, transcendentals=0
        ),
        name="forward",
    )(x, operators, block)


def backward_kernel(q_ref, block_ref, x_ref, enter_ref, w_ref, z_high, z_low, carried):
    @pl.when(pl.program_id(0) == 0)
    def _():
        nb = block_ref.shape[1]
        reverse = jnp.zeros((q_ref.shape[2], 1), F32)
        for b in reversed(range(nb)):
            q = q_ref[0, b * BLK : (b + 1) * BLK, :].astype(F32)
            out = jnp.dot(q.T, block_ref[0, b, :BLK, :], precision=HIGHEST, preferred_element_type=F32)
            out = out - reverse * block_ref[0, b, BLK : BLK + 1, :]
            z = out[:, :BLK]
            high = z.astype(BF16)
            z_high[:, b * BLK : (b + 1) * BLK] = high
            z_low[:, b * BLK : (b + 1) * BLK] = (z - high.astype(F32)).astype(BF16)
            reverse = out[:, BLK : BLK + 1]
        carried[...] = jnp.broadcast_to(reverse, carried.shape)

    x = x_ref[:, 0].reshape(z_high.shape[1], x_ref.shape[3])
    w = jnp.dot(z_high[...], x, preferred_element_type=F32)
    w = w + jnp.dot(z_low[...], x, preferred_element_type=F32)
    w = w - carried[:, 0:1] * enter_ref[0, 0:1, :]
    w_ref[...] = w.astype(w_ref.dtype)


def backward(f, q, block, x, enter):
    n, _, rows, width = x.shape
    hours, rank = q.shape[1:]
    nb = hours // BLK
    return pl.pallas_call(
        backward_kernel,
        grid=(width // NCHUNK,),
        in_specs=[
            pl.BlockSpec((1, hours, rank), lambda i: (1 - f, 0, 0)),
            pl.BlockSpec((1, nb, BLK + 8, BLK + 128), lambda i: (f, 0, 0, 0)),
            pl.BlockSpec((n, 1, rows, NCHUNK), lambda i: (0, f, 0, i)),
            pl.BlockSpec((1, 8, NCHUNK), lambda i: (f, 0, i)),
        ],
        out_specs=pl.BlockSpec((rank, NCHUNK), lambda i: (0, i)),
        out_shape=jax.ShapeDtypeStruct((rank, width), BF16),
        scratch_shapes=[
            pltpu.VMEM((rank, hours), BF16),
            pltpu.VMEM((rank, hours), BF16),
            pltpu.VMEM((rank, 128), F32),
        ],
        compiler_params=pltpu.CompilerParams(vmem_limit_bytes=24 << 20),
        cost_estimate=pl.CostEstimate(
            flops=4 * hours * width * rank, bytes_accessed=2 * hours * width, transcendentals=0
        ),
        name="backward",
    )(q, block, x, enter)


def middle_kernel(q_ref, out_ref):
    left = q_ref[0].astype(F32).T.astype(BF16)
    out_ref[...] = jnp.dot(left, q_ref[1], preferred_element_type=F32)


def cross(q):
    _, hours, rank = q.shape
    return pl.pallas_call(
        middle_kernel,
        out_shape=jax.ShapeDtypeStruct((rank, rank), F32),
        in_specs=[pl.BlockSpec(memory_space=pltpu.VMEM)],
        out_specs=pl.BlockSpec(memory_space=pltpu.VMEM),
        compiler_params=pltpu.CompilerParams(vmem_limit_bytes=8 << 20),
        cost_estimate=pl.CostEstimate(flops=2 * hours * rank * rank, bytes_accessed=2 * q.size, transcendentals=0),
        name="cross",
    )(q)


def all_to_all(x, axis, groups=None):
    return lax.all_to_all(x, axis, split_axis=0, concat_axis=0, tiled=True, axis_index_groups=groups)


def pick(x, i):
    return lax.dynamic_index_in_dim(x, i, 0, keepdims=False)


def shifted(x, by):
    n = lax.axis_size("tm")
    return lax.ppermute(x, "tm", [(i, (i + by) % n) for i in range(n)])


def entering(end, gain, start):
    message = jnp.concatenate([end, jnp.broadcast_to(gain[:, None], end.shape), jnp.zeros((4, end.shape[1]), F32)])
    i = lax.axis_index("tm")
    total, so_far = jnp.zeros_like(end), jnp.ones_like(end)
    for d in range(1, lax.axis_size("tm")):
        got = shifted(message, d)
        total = total + jnp.where(i >= d, so_far * got[:2], 0.0)
        so_far = so_far * jnp.where(i >= d, got[2:4], 1.0)
    return total + so_far * start


def across(x):
    return lax.ppermute(x, "grid", [(g, g ^ 1) for g in range(Y * Z * C)])


def summed_over_grid(p, *held):
    core = lax.axis_index("grid") % C
    _, hours, rank = p.shape
    n = Y * Z
    rows = hours // (n * C)
    groups = [[k * C + c for k in range(n)] for c in range(C)]
    p = p.reshape(2, C, n * rows, rank)
    own = lax.dynamic_index_in_dim(p, core, 1, keepdims=False)
    other = lax.dynamic_index_in_dim(p, 1 - core, 1, keepdims=False)
    p = (own + across(other)).astype(BF16).reshape(2, n, rows, rank)
    p, *held = lax.optimization_barrier((p.transpose(1, 0, 2, 3), *held))
    p = all_to_all(p, "grid", groups)
    q = p.astype(F32).sum(axis=0).astype(BF16)
    q = all_to_all(jnp.broadcast_to(q, p.shape), "grid", groups)
    q = q.transpose(1, 0, 2, 3).reshape(2, n * rows, rank)
    other = across(q)
    first = core == 0
    low, high = jnp.where(first, q, other), jnp.where(first, other, q)
    q = jnp.stack([low, high], axis=1).reshape(2, hours, rank)
    return q, *held


def summed_over_hours(w):
    n = lax.axis_size("tm")
    rank, width = w.shape
    w = w.reshape(n, rank // n, width)
    i, half = lax.axis_index("tm"), width // 2
    own, ahead, far, back = (pick(w, (i + k) % n) for k in range(n))
    add = lambda a, b: a.astype(F32) + b.astype(F32)
    up = shifted(far[:, :half], 1)
    down = shifted(far[:, half:], n - 1)
    from_below = shifted(ahead[:, half:], 1)
    from_above = shifted(back[:, :half], n - 1)
    up = shifted(add(up, ahead[:, :half]).astype(BF16), 1)
    down = shifted(add(down, back[:, half:]).astype(BF16), n - 1)
    left = add(own[:, :half], from_above) + up.astype(F32)
    right = add(own[:, half:], from_below) + down.astype(F32)
    return jnp.concatenate([left, right], axis=1)


def per_device(x0, x1, fading, starting, operator0, operator1):
    grid = lax.axis_size("grid")
    rows, points = x0.shape
    width, hours = points // grid, rows * grid
    scale = (hours * lax.axis_size("tm")) ** -0.5
    x = all_to_all(pack(x0, x1, grid), "grid")
    block, since_start, to_end, gain = decay_blocks(fading)
    operators = jnp.stack([operator0, operator1])
    start = []
    for f in range(2):
        rest, parts = starting[f], []
        for _ in range(3):
            parts.append(rest.astype(BF16))
            rest = rest - parts[-1].astype(F32)
        start.append(jnp.dot(jnp.stack(parts), operators[f], preferred_element_type=F32).sum(axis=0))
    start = jnp.stack(start)
    p, end = forward(x, operators, block)
    p = p - since_start[:, :, None] * entering(end[:, 0], gain, start)[:, None]
    q, x = summed_over_grid(p, x)
    weight = to_end.reshape(2, grid, rows).transpose(1, 0, 2)[..., None]
    mean = entering((x.astype(F32) * weight).sum(axis=(0, 2)), gain, starting)
    mean = jnp.broadcast_to(mean[:, None], (2, 8, width))
    w1 = backward(1, q, block, x, mean)
    wetness = summed_over_hours(w1) * scale
    core = lax.axis_index("grid") % C
    halves = cross(q).reshape(C, -1, q.shape[2])
    sent = pick(halves, core).astype(BF16)
    half = sent.astype(F32)
    for d in range(1, lax.axis_size("tm")):
        half = half + shifted(sent, d).astype(F32)
    other = across(half)
    middle = jnp.concatenate([jnp.where(core == 0, half, other), jnp.where(core == 0, other, half)])
    w0 = backward(0, q, block, x, mean)
    warmth = summed_over_hours(w0) * scale
    return warmth, wetness, middle * scale


def solution(mesh):
    return jax.shard_map(
        per_device,
        mesh=mesh,
        in_specs=(
            P(("tm", "grid"), None),
            P(("tm", "grid"), None),
            P(None, "tm"),
            P(None, "grid"),
            P("grid", None),
            P("grid", None),
        ),
        out_specs=(P("tm", "grid"), P("tm", "grid"), P()),
        check_vma=False,
    )
```

```python
import jax
import jax.numpy as jnp
from jax import lax
from jax.experimental import pallas as pl
from jax.experimental.pallas import tpu as pltpu
from jax.sharding import PartitionSpec as P


BLK = 256
NCHUNK = 512
Y, Z, C = 4, 4, 2
F32, BF16 = jnp.float32, jnp.bfloat16
HIGHEST = lax.Precision.HIGHEST


def decay_blocks(fading):
    nb = fading.shape[1] // BLK
    a = fading.reshape(2, nb, BLK)
    log_a = jnp.log(a)
    inclusive = jnp.cumsum(log_a, axis=2)
    before = jnp.concatenate([jnp.zeros((2, nb, 1), F32), inclusive, jnp.zeros((2, nb, 7), F32)], axis=2)
    rows, cols = BLK + 8, BLK + 128
    r = lax.broadcasted_iota(jnp.int32, (rows, cols), 0)
    c = lax.broadcasted_iota(jnp.int32, (rows, cols), 1)
    pad = lambda v: jnp.pad(v, ((0, 0), (0, 0), (0, 128)))
    spread = before[..., :, None] - pad(inclusive)[..., None, :]
    gain = pad(1.0 - a)[..., None, :]
    gain = jnp.where(c == BLK, 1.0, gain)
    weight = jnp.exp(jnp.minimum(spread, 0.0)) * gain
    weight = jnp.where((c < jnp.minimum(r, BLK)) | (c == BLK), weight, 0.0)
    sign = jnp.where((r < BLK) == (c < BLK), -1.0, 1.0)
    block = jnp.where(r == c, jnp.where(r < BLK, 1.0, sign * weight), sign * weight)
    block = jnp.where(r <= BLK, block, 0.0)
    total = inclusive[..., -1]
    ahead = jnp.cumsum(total, axis=1) - total
    since_start = jnp.exp(ahead[..., None] + before[..., :BLK]).reshape(2, nb * BLK)
    behind = jnp.cumsum(total[:, ::-1], axis=1)[:, ::-1] - total
    to_end = jnp.exp(behind[..., None] + inclusive[..., -1:] - inclusive) * (1.0 - a)
    return block, since_start, to_end.reshape(2, nb * BLK), jnp.exp(total.sum(axis=1))


def pack_kernel(x0_ref, x1_ref, out_ref):
    out_ref[0, 0] = x0_ref[...]
    out_ref[0, 1] = x1_ref[...]


def pack(x0, x1, n):
    rows, points = x0.shape
    width = points // n
    return pl.pallas_call(
        pack_kernel,
        grid=(n,),
        in_specs=[pl.BlockSpec((rows, width), lambda i: (0, i))] * 2,
        out_specs=pl.BlockSpec((1, 2, rows, width), lambda i: (i, 0, 0, 0)),
        out_shape=jax.ShapeDtypeStruct((n, 2, rows, width), x0.dtype),
        compiler_params=pltpu.CompilerParams(vmem_limit_bytes=16 << 20),
        cost_estimate=pl.CostEstimate(flops=0, bytes_accessed=8 * x0.size, transcendentals=0),
        name="pack",
    )(x0, x1)


def forward_kernel(x_ref, op_ref, block_ref, p_ref, end_ref, state):
    b = pl.program_id(1)

    @pl.when(b == 0)
    def _():
        state[...] = jnp.zeros_like(state)

    x = x_ref[:, 0].reshape(BLK, x_ref.shape[3])
    y = jnp.dot(x, op_ref[0], preferred_element_type=F32)
    out = jnp.dot(block_ref[0, 0, :, :BLK], y, precision=HIGHEST, preferred_element_type=F32)
    out = out - block_ref[0, 0, :, BLK : BLK + 1] * state[0:1, :]
    p_ref[0] = out[:BLK]
    state[...] = out[BLK:]
    end_ref[0] = out[BLK:]


def forward(x, operators, block):
    n, _, rows, width = x.shape
    rank = operators.shape[2]
    hours = n * rows
    nb, per = hours // BLK, BLK // rows
    return pl.pallas_call(
        forward_kernel,
        grid=(2, nb),
        in_specs=[
            pl.BlockSpec((per, 1, rows, width), lambda f, b: (b, f, 0, 0)),
            pl.BlockSpec((1, width, rank), lambda f, b: (f, 0, 0)),
            pl.BlockSpec((1, 1, BLK + 8, BLK + 128), lambda f, b: (f, b, 0, 0)),
        ],
        out_specs=[
            pl.BlockSpec((1, BLK, rank), lambda f, b: (f, b, 0)),
            pl.BlockSpec((1, 8, rank), lambda f, b: (f, 0, 0)),
        ],
        out_shape=[
            jax.ShapeDtypeStruct((2, hours, rank), F32),
            jax.ShapeDtypeStruct((2, 8, rank), F32),
        ],
        scratch_shapes=[pltpu.VMEM((8, rank), F32)],
        compiler_params=pltpu.CompilerParams(vmem_limit_bytes=24 << 20),
        cost_estimate=pl.CostEstimate(
            flops=4 * hours * width * rank, bytes_accessed=4 * hours * width, transcendentals=0
        ),
        name="forward",
    )(x, operators, block)


def backward_kernel(q_ref, block_ref, x_ref, enter_ref, w_ref, z_high, z_low, carried):
    @pl.when(pl.program_id(0) == 0)
    def _():
        nb = block_ref.shape[1]
        reverse = jnp.zeros((q_ref.shape[2], 1), F32)
        for b in reversed(range(nb)):
            q = q_ref[0, b * BLK : (b + 1) * BLK, :].astype(F32)
            out = jnp.dot(q.T, block_ref[0, b, :BLK, :], precision=HIGHEST, preferred_element_type=F32)
            out = out - reverse * block_ref[0, b, BLK : BLK + 1, :]
            z = out[:, :BLK]
            high = z.astype(BF16)
            z_high[:, b * BLK : (b + 1) * BLK] = high
            z_low[:, b * BLK : (b + 1) * BLK] = (z - high.astype(F32)).astype(BF16)
            reverse = out[:, BLK : BLK + 1]
        carried[...] = jnp.broadcast_to(reverse, carried.shape)

    x = x_ref[:, 0].reshape(z_high.shape[1], x_ref.shape[3])
    w = jnp.dot(z_high[...], x, preferred_element_type=F32)
    w = w + jnp.dot(z_low[...], x, preferred_element_type=F32)
    w = w - carried[:, 0:1] * enter_ref[0, 0:1, :]
    w_ref[...] = w.astype(w_ref.dtype)


def backward(f, q, block, x, enter):
    n, _, rows, width = x.shape
    hours, rank = q.shape[1:]
    nb = hours // BLK
    return pl.pallas_call(
        backward_kernel,
        grid=(width // NCHUNK,),
        in_specs=[
            pl.BlockSpec((1, hours, rank), lambda i: (1 - f, 0, 0)),
            pl.BlockSpec((1, nb, BLK + 8, BLK + 128), lambda i: (f, 0, 0, 0)),
            pl.BlockSpec((n, 1, rows, NCHUNK), lambda i: (0, f, 0, i)),
            pl.BlockSpec((1, 8, NCHUNK), lambda i: (f, 0, i)),
        ],
        out_specs=pl.BlockSpec((rank, NCHUNK), lambda i: (0, i)),
        out_shape=jax.ShapeDtypeStruct((rank, width), BF16),
        scratch_shapes=[
            pltpu.VMEM((rank, hours), BF16),
            pltpu.VMEM((rank, hours), BF16),
            pltpu.VMEM((rank, 128), F32),
        ],
        compiler_params=pltpu.CompilerParams(vmem_limit_bytes=24 << 20),
        cost_estimate=pl.CostEstimate(
            flops=4 * hours * width * rank, bytes_accessed=2 * hours * width, transcendentals=0
        ),
        name="backward",
    )(q, block, x, enter)


def middle_kernel(q_ref, out_ref):
    left = q_ref[0].astype(F32).T.astype(BF16)
    out_ref[...] = jnp.dot(left, q_ref[1], preferred_element_type=F32)


def cross(q):
    _, hours, rank = q.shape
    return pl.pallas_call(
        middle_kernel,
        out_shape=jax.ShapeDtypeStruct((rank, rank), F32),
        in_specs=[pl.BlockSpec(memory_space=pltpu.VMEM)],
        out_specs=pl.BlockSpec(memory_space=pltpu.VMEM),
        compiler_params=pltpu.CompilerParams(vmem_limit_bytes=8 << 20),
        cost_estimate=pl.CostEstimate(flops=2 * hours * rank * rank, bytes_accessed=2 * q.size, transcendentals=0),
        name="cross",
    )(q)


def all_to_all(x, axis, groups=None):
    return lax.all_to_all(x, axis, split_axis=0, concat_axis=0, tiled=True, axis_index_groups=groups)


def pick(x, i):
    return lax.dynamic_index_in_dim(x, i, 0, keepdims=False)


def shifted(x, by):
    n = lax.axis_size("tm")
    return lax.ppermute(x, "tm", [(i, (i + by) % n) for i in range(n)])


def entering(end, gain, start):
    message = jnp.concatenate([end, jnp.broadcast_to(gain[:, None], end.shape)])
    i = lax.axis_index("tm")
    total, so_far = jnp.zeros_like(end), jnp.ones_like(end)
    for d in range(1, lax.axis_size("tm")):
        got = shifted(message, d)
        total = total + jnp.where(i >= d, so_far * got[:2], 0.0)
        so_far = so_far * jnp.where(i >= d, got[2:4], 1.0)
    return total + so_far * start


def across(x):
    return lax.ppermute(x, "grid", [(g, g ^ 1) for g in range(Y * Z * C)])


def summed_over_grid(p, *held):
    core = lax.axis_index("grid") % C
    _, hours, rank = p.shape
    n = Y * Z
    rows = hours // (n * C)
    groups = [[k * C + c for k in range(n)] for c in range(C)]
    p = p.reshape(2, C, n * rows, rank)
    own = lax.dynamic_index_in_dim(p, core, 1, keepdims=False)
    other = lax.dynamic_index_in_dim(p, 1 - core, 1, keepdims=False)
    p = (own + across(other)).astype(BF16).reshape(2, n, rows, rank)
    p, *held = lax.optimization_barrier((p.transpose(1, 0, 2, 3), *held))
    p = all_to_all(p, "grid", groups)
    q = p.astype(F32).sum(axis=0).astype(BF16)
    q = all_to_all(jnp.broadcast_to(q, p.shape), "grid", groups)
    q = q.transpose(1, 0, 2, 3).reshape(2, n * rows, rank)
    other = across(q)
    first = core == 0
    low, high = jnp.where(first, q, other), jnp.where(first, other, q)
    q = jnp.stack([low, high], axis=1).reshape(2, hours, rank)
    return q, *held


def summed_over_hours(w):
    n = lax.axis_size("tm")
    rank, width = w.shape
    w = w.reshape(n, rank // n, width)
    i, half = lax.axis_index("tm"), width // 2
    own, ahead, far, back = (pick(w, (i + k) % n) for k in range(n))
    add = lambda a, b: a.astype(F32) + b.astype(F32)
    up = shifted(far[:, :half], 1)
    down = shifted(far[:, half:], n - 1)
    from_below = shifted(ahead[:, half:], 1)
    from_above = shifted(back[:, :half], n - 1)
    up = shifted(add(up, ahead[:, :half]).astype(BF16), 1)
    down = shifted(add(down, back[:, half:]).astype(BF16), n - 1)
    left = add(own[:, :half], from_above) + up.astype(F32)
    right = add(own[:, half:], from_below) + down.astype(F32)
    return jnp.concatenate([left, right], axis=1)


def per_device(x0, x1, fading, starting, operator0, operator1):
    grid = lax.axis_size("grid")
    rows, points = x0.shape
    width, hours = points // grid, rows * grid
    scale = (hours * lax.axis_size("tm")) ** -0.5
    block, since_start, to_end, gain = decay_blocks(fading)
    operators = jnp.stack([operator0, operator1])
    start = []
    for f in range(2):
        rest, parts = starting[f], []
        for _ in range(3):
            parts.append(rest.astype(BF16))
            rest = rest - parts[-1].astype(F32)
        start.append(jnp.dot(jnp.stack(parts), operators[f], preferred_element_type=F32).sum(axis=0))
    start = jnp.stack(start)
    weight = to_end.reshape(2, grid, rows).transpose(1, 0, 2)[..., None]
    ready = (block, since_start, weight, gain, start, operators)
    packed, ready = lax.optimization_barrier((pack(x0, x1, grid), ready))
    x = all_to_all(packed, "grid")
    x, ready = lax.optimization_barrier((x, ready))
    block, since_start, weight, gain, start, operators = ready
    p, end = forward(x, operators, block)
    p = p - since_start[:, :, None] * entering(end[:, 0], gain, start)[:, None]
    q, x = summed_over_grid(p, x)
    mean = entering((x.astype(F32) * weight).sum(axis=(0, 2)), gain, starting)
    mean = jnp.broadcast_to(mean[:, None], (2, 8, width))
    w1 = backward(1, q, block, x, mean)
    wetness = summed_over_hours(w1) * scale
    core = lax.axis_index("grid") % C
    halves = cross(q).reshape(C, -1, q.shape[2])
    sent = pick(halves, core).astype(BF16)
    half = sent.astype(F32)
    for d in range(1, lax.axis_size("tm")):
        half = half + shifted(sent, d).astype(F32)
    other = across(half)
    middle = jnp.concatenate([jnp.where(core == 0, half, other), jnp.where(core == 0, other, half)])
    w0 = backward(0, q, block, x, mean)
    warmth = summed_over_hours(w0) * scale
    return warmth, wetness, middle * scale


def solution(mesh):
    return jax.shard_map(
        per_device,
        mesh=mesh,
        in_specs=(
            P(("tm", "grid"), None),
            P(("tm", "grid"), None),
            P(None, "tm"),
            P(None, "grid"),
            P("grid", None),
            P("grid", None),
        ),
        out_specs=(P("tm", "grid"), P("tm", "grid"), P()),
        check_vma=False,
    )
```

```python
import jax
import jax.numpy as jnp
from jax import lax
from jax.experimental import pallas as pl
from jax.experimental.pallas import tpu as pltpu
from jax.sharding import PartitionSpec as P


BLK = 256
NCHUNK = 512
Y, Z, C = 4, 4, 2
F32, BF16 = jnp.float32, jnp.bfloat16
HIGHEST = lax.Precision.HIGHEST
MIB = 1 << 20


def thirds(v):
    high = v.astype(BF16)
    v = v - high.astype(F32)
    middle = v.astype(BF16)
    return high, middle, (v - middle.astype(F32)).astype(BF16)


def prepare_kernel(x0_ref, x1_ref, fading_ref, out_ref, block_ref, since_ref, to_end_ref, gain_ref, sems):
    n, _, _, width = out_ref.shape

    def copies():
        for i in range(n):
            for f, x_ref in enumerate((x0_ref, x1_ref)):
                yield pltpu.make_async_copy(x_ref.at[:, pl.ds(i * width, width)], out_ref.at[i, f], sems.at[2 * i + f])

    for copy in copies():
        copy.start()
    a = fading_ref[...]
    log_a = jnp.log(a)
    r = lax.broadcasted_iota(jnp.int32, (BLK, BLK), 0)
    c = lax.broadcasted_iota(jnp.int32, (BLK, BLK), 1)
    upto = jnp.where(r <= c, 1.0, 0.0)
    inclusive = jnp.dot(log_a, upto, precision=HIGHEST, preferred_element_type=F32)
    exclusive = jnp.where(lax.broadcasted_iota(jnp.int32, a.shape, 1) == 0, 0.0, pltpu.roll(inclusive, 1, 1))
    column = exclusive.T
    fresh = 1.0 - a
    total = inclusive[:, BLK - 1 : BLK]
    nb = a.shape[0] // 2
    for f in range(2):
        sums = [total[f * nb + b : f * nb + b + 1] for b in range(nb)]
        ahead = jnp.zeros_like(sums[0])
        for b in range(nb):
            k = f * nb + b
            row = slice(k, k + 1)
            weight = jnp.exp(jnp.minimum(column[:, k : k + 1] - inclusive[row], 0.0)) * fresh[row]
            block_ref[k, :BLK, :BLK] = jnp.where(r == c, 1.0, jnp.where(c < r, -weight, 0.0))
            block_ref[k, :BLK, BLK:] = jnp.broadcast_to(jnp.exp(column[:, k : k + 1]), (BLK, 128))
            last = jnp.exp(sums[b] - inclusive[row]) * fresh[row]
            block_ref[k, BLK:, :BLK] = jnp.broadcast_to(last, (8, BLK))
            block_ref[k, BLK:, BLK:] = jnp.broadcast_to(-jnp.exp(sums[b]), (8, 128))
            behind = sum(sums[b + 1 :], jnp.zeros_like(ahead))
            since_ref[row] = jnp.exp(ahead + exclusive[row])
            to_end_ref[row] = jnp.exp(behind + (sums[b] - inclusive[row])) * fresh[row]
            ahead = ahead + sums[b]
        gain_ref[f : f + 1] = jnp.broadcast_to(jnp.exp(ahead), (1, BLK))
    for copy in copies():
        copy.wait()


def prepare(x0, x1, fading, n):
    rows, points = x0.shape
    width = points // n
    count = fading.size // BLK
    whole = pl.BlockSpec(memory_space=pltpu.VMEM)
    return pl.pallas_call(
        prepare_kernel,
        in_specs=[pl.BlockSpec(memory_space=pl.ANY), pl.BlockSpec(memory_space=pl.ANY), whole],
        out_specs=[pl.BlockSpec(memory_space=pl.ANY), whole, whole, whole, whole],
        out_shape=[
            jax.ShapeDtypeStruct((n, 2, rows, width), x0.dtype),
            jax.ShapeDtypeStruct((count, BLK + 8, BLK + 128), F32),
            jax.ShapeDtypeStruct((count, BLK), F32),
            jax.ShapeDtypeStruct((count, BLK), F32),
            jax.ShapeDtypeStruct((2, BLK), F32),
        ],
        scratch_shapes=[pltpu.SemaphoreType.DMA((2 * n,))],
        compiler_params=pltpu.CompilerParams(vmem_limit_bytes=24 * MIB),
        cost_estimate=pl.CostEstimate(flops=0, bytes_accessed=8 * x0.size, transcendentals=0),
        name="prepare",
    )(x0, x1, fading.reshape(count, BLK))


def forward_kernel(place_ref, x_ref, op_ref, block_ref, start_ref, own_ref, other_ref, end_ref, begin_ref, y_ref):
    f = pl.program_id(0)
    n, _, rows, width = x_ref.shape
    hours = n * rows
    nb = hours // BLK
    y_ref[...] = jnp.dot(x_ref[:, 0].reshape(hours, width), op_ref[0], preferred_element_type=F32)
    state = jnp.zeros((1, op_ref.shape[2]), F32)
    gain = jnp.ones((1, 1), F32)
    per = BLK // rows
    for b in range(nb):
        block = block_ref[b]
        out = jnp.dot(block[:, :BLK], y_ref[b * BLK : (b + 1) * BLK], precision=HIGHEST, preferred_element_type=F32)
        out = out - block[:, BLK : BLK + 1] * state
        part = out[:BLK].reshape(per, rows, out.shape[1])
        half, at = divmod(b, nb // 2)

        @pl.when(place_ref[0] == half)
        def _():
            own_ref[at * per : (at + 1) * per, 0] = part

        @pl.when(place_ref[0] != half)
        def _():
            other_ref[at * per : (at + 1) * per, 0] = part

        state = out[BLK : BLK + 1]
    start = jnp.concatenate([part.astype(F32) for part in thirds(start_ref[0])] + [jnp.zeros((5, width), F32)])
    begin = jnp.dot(start.astype(BF16), op_ref[0], preferred_element_type=F32)
    begin = begin[0:1] + begin[1:2] + begin[2:3]
    for k in range(2):

        @pl.when(f == k)
        def _():
            end_ref[k : k + 1] = state
            begin_ref[k : k + 1] = begin


def forward(place, x, operators, block, starting):
    n, _, rows, width = x.shape
    rank = operators.shape[2]
    hours = n * rows
    nb = hours // BLK
    half = jax.ShapeDtypeStruct((n // 2, 2, rows, rank), F32)
    half_spec = pl.BlockSpec((n // 2, 1, rows, rank), lambda f: (0, f, 0, 0))
    pair, pair_spec = jax.ShapeDtypeStruct((2, rank), F32), pl.BlockSpec((2, rank), lambda f: (0, 0))
    return pl.pallas_call(
        forward_kernel,
        grid=(2,),
        in_specs=[
            pl.BlockSpec(memory_space=pltpu.SMEM),
            pl.BlockSpec((n, 1, rows, width), lambda f: (0, f, 0, 0)),
            pl.BlockSpec((1, width, rank), lambda f: (f, 0, 0)),
            pl.BlockSpec((nb, BLK + 8, BLK + 128), lambda f: (f, 0, 0)),
            pl.BlockSpec((1, 1, width), lambda f: (f, 0, 0)),
        ],
        out_specs=[half_spec, half_spec, pair_spec, pair_spec],
        out_shape=[half, half, pair, pair],
        scratch_shapes=[pltpu.VMEM((hours, rank), F32)],
        compiler_params=pltpu.CompilerParams(vmem_limit_bytes=36 * MIB),
        cost_estimate=pl.CostEstimate(
            flops=4 * hours * width * rank, bytes_accessed=4 * hours * width, transcendentals=0
        ),
        name="forward",
    )(place, x, operators, block, starting)


def backward_kernel(
    place_ref, own_ref, other_ref, block_ref, x_ref, enter_ref, send0_ref, keep0_ref, send1_ref, keep1_ref, z_high, z_low, carried
):
    step = pl.program_id(0)
    rank = own_ref.shape[3]
    quarter = rank // 4

    @pl.when(step == 0)
    def _():
        nb = block_ref.shape[0]
        rows = own_ref.shape[2]
        per = BLK // rows
        swap = place_ref[1]
        reverse = jnp.zeros((rank, 1), F32)

        def placed(ref, value, cols):
            for d in range(4):
                at = pl.multiple_of(jnp.bitwise_xor(d, swap) * quarter, quarter)
                ref[pl.ds(at, quarter), cols] = value[d * quarter : (d + 1) * quarter]

        for b in reversed(range(nb)):
            half, at = divmod(b, nb // 2)
            own = own_ref[at * per : (at + 1) * per, 0].reshape(BLK, rank)
            other = other_ref[at * per : (at + 1) * per, 0].reshape(BLK, rank)
            q = jnp.where(place_ref[0] == half, own.astype(F32), other.astype(F32)).T.astype(BF16)
            out = jnp.zeros((rank, BLK + 128), F32)
            for part in reversed(thirds(block_ref[b, :BLK])):
                out = out + jnp.dot(q, part, preferred_element_type=F32)
            out = out - reverse * block_ref[b, BLK : BLK + 1, :]
            z = out[:, :BLK]
            high = z.astype(BF16)
            cols = slice(b * BLK, (b + 1) * BLK)
            placed(z_high, high, cols)
            placed(z_low, (z - high.astype(F32)).astype(BF16), cols)
            reverse = out[:, BLK : BLK + 1]
        placed(carried, jnp.broadcast_to(reverse, carried.shape), slice(0, carried.shape[1]))

    x = x_ref[:, 0].reshape(z_high.shape[1], x_ref.shape[3])
    w = jnp.dot(z_high[...], x, preferred_element_type=F32)
    w = w + jnp.dot(z_low[...], x, preferred_element_type=F32)
    w = w - carried[:, 0:1] * enter_ref[0]
    w = [w[k * quarter : (k + 1) * quarter].astype(BF16) for k in range(4)]

    @pl.when(step < pl.num_programs(0) // 2)
    def _():
        send0_ref[:quarter], send0_ref[quarter:] = w[1], w[2]
        keep0_ref[:quarter], keep0_ref[quarter:] = w[0], w[3]

    @pl.when(step >= pl.num_programs(0) // 2)
    def _():
        send1_ref[:quarter], send1_ref[quarter:] = w[2], w[3]
        keep1_ref[:quarter], keep1_ref[quarter:] = w[0], w[1]


def backward(f, place, own, other, block, x, enter):
    n, _, rows, width = x.shape
    hours, rank = n * rows, own.shape[3]
    nb = hours // BLK
    steps = width // NCHUNK // 2
    q_spec = pl.BlockSpec((n // 2, 1, rows, rank), lambda i: (0, 1 - f, 0, 0))
    left = pl.BlockSpec((rank // 2, NCHUNK), lambda i: (0, jnp.minimum(i, steps - 1)))
    right = pl.BlockSpec((rank // 2, NCHUNK), lambda i: (0, jnp.maximum(i - steps, 0)))
    piece = jax.ShapeDtypeStruct((rank // 2, width // 2), BF16)
    return pl.pallas_call(
        backward_kernel,
        grid=(2 * steps,),
        in_specs=[
            pl.BlockSpec(memory_space=pltpu.SMEM),
            q_spec,
            q_spec,
            pl.BlockSpec((nb, BLK + 8, BLK + 128), lambda i: (f, 0, 0)),
            pl.BlockSpec((n, 1, rows, NCHUNK), lambda i: (0, f, 0, i)),
            pl.BlockSpec((1, 1, NCHUNK), lambda i: (f, 0, i)),
        ],
        out_specs=[left, left, right, right],
        out_shape=[piece] * 4,
        scratch_shapes=[
            pltpu.VMEM((rank, hours), BF16),
            pltpu.VMEM((rank, hours), BF16),
            pltpu.VMEM((rank, 128), F32),
        ],
        compiler_params=pltpu.CompilerParams(vmem_limit_bytes=54 * MIB),
        cost_estimate=pl.CostEstimate(
            flops=4 * hours * width * rank, bytes_accessed=2 * hours * width, transcendentals=0
        ),
        name="backward",
    )(place, own, other, block, x, enter[:, None])


def cross_kernel(place_ref, own_ref, other_ref, out_ref):
    n, _, rows, rank = own_ref.shape
    out = jnp.zeros(out_ref.shape, F32)
    for ref in (own_ref, other_ref):
        left = ref[:, 0].reshape(n * rows, rank).astype(F32).T.astype(BF16)
        out = out + jnp.dot(left, ref[:, 1].reshape(n * rows, rank), preferred_element_type=F32)
    out_ref[...] = out


def cross(place, own, other):
    rank = own.shape[3]
    whole = pl.BlockSpec(memory_space=pltpu.VMEM)
    return pl.pallas_call(
        cross_kernel,
        out_shape=jax.ShapeDtypeStruct((rank, rank), F32),
        in_specs=[pl.BlockSpec(memory_space=pltpu.SMEM), whole, whole],
        out_specs=whole,
        compiler_params=pltpu.CompilerParams(vmem_limit_bytes=8 * MIB),
        cost_estimate=pl.CostEstimate(flops=2 * own.size * rank, bytes_accessed=4 * own.size, transcendentals=0),
        name="cross",
    )(place, own, other)


def all_to_all(x, axis, groups=None):
    return lax.all_to_all(x, axis, split_axis=0, concat_axis=0, tiled=True, axis_index_groups=groups)


def shifted(x, by):
    n = lax.axis_size("tm")
    return lax.ppermute(x, "tm", [(i, (i + by) % n) for i in range(n)])


def paired(x, by):
    return lax.ppermute(x, "tm", [(i, i ^ by) for i in range(lax.axis_size("tm"))])


def across(x):
    return lax.ppermute(x, "grid", [(g, g ^ 1) for g in range(Y * Z * C)])


def entering(end, gain, start):
    message = jnp.concatenate([end, jnp.broadcast_to(gain, end.shape)])
    i = lax.axis_index("tm")
    total, so_far = jnp.zeros_like(end), jnp.ones_like(end)
    for d in range(1, lax.axis_size("tm")):
        got = shifted(message, d)
        total = total + jnp.where(i >= d, so_far * got[:2], 0.0)
        so_far = so_far * jnp.where(i >= d, got[2:4], 1.0)
    return total + so_far * start


def summed_over_hours(pieces):
    send0, keep0, send1, keep1 = pieces
    q = send0.shape[0] // 2
    wide = lambda v: v.astype(F32)
    got0 = paired(send0, 1)
    got1 = paired(send1, 3)
    last0 = paired((wide(keep0[q:]) + wide(got0[q:])).astype(BF16), 3)
    last1 = paired((wide(keep1[q:]) + wide(got1[:q])).astype(BF16), 1)
    left = wide(keep0[:q]) + wide(got0[:q]) + wide(last0)
    right = wide(keep1[:q]) + wide(got1[q:]) + wide(last1)
    return jnp.concatenate([left, right], axis=1)


def per_device(x0, x1, fading, starting, operator0, operator1):
    grid = lax.axis_size("grid")
    rows, _ = x0.shape
    hours = rows * grid
    scale = (hours * lax.axis_size("tm")) ** -0.5
    core = lax.axis_index("grid") % C
    place = jnp.stack([core, lax.axis_index("tm")]).astype(jnp.int32)
    n = grid // C
    groups = [[k * C + c for k in range(n)] for c in range(C)]
    packed, *tables = prepare(x0, x1, fading, grid)
    operators = jnp.stack([operator0, operator1])
    rest = (tables, operators, place, starting, starting[:, None])
    packed, rest = lax.optimization_barrier((packed, rest))
    x = all_to_all(packed, "grid")
    x, (tables, operators, place, starting, start_rows) = lax.optimization_barrier((x, rest))
    block, since, to_end, gain = tables
    own, other, end, begin = forward(place, x, operators, block, start_rows)
    enter = entering(end, gain[:, :1], begin)
    enter = enter + across(enter)
    since = lax.dynamic_index_in_dim(since.reshape(2, C, n, rows), core, 1, keepdims=False).transpose(1, 0, 2)
    p = own + across(other) - since[..., None] * enter[None, :, None]
    p, x = lax.optimization_barrier((p.astype(BF16), x))
    p = all_to_all(p, "grid", groups)
    q = p.astype(F32).sum(axis=0).astype(BF16)
    q_own = all_to_all(jnp.broadcast_to(q, p.shape), "grid", groups)
    q_other = across(q_own)
    weight = to_end.reshape(2, grid, rows).transpose(1, 0, 2)[..., None]
    mean = entering((x.astype(F32) * weight).sum(axis=(0, 2)), gain[:, :1], starting)
    w1 = backward(1, place, q_own, q_other, block, x, mean)
    wetness = summed_over_hours(w1) * scale
    sent = lax.dynamic_index_in_dim(cross(place, q_own, q_other).reshape(C, -1, q.shape[2]), core, 0, keepdims=False)
    sent = sent.astype(BF16)
    half = sent.astype(F32)
    for d in range(1, lax.axis_size("tm")):
        half = half + shifted(sent, d).astype(F32)
    partner = across(half)
    middle = jnp.concatenate([jnp.where(core == 0, half, partner), jnp.where(core == 0, partner, half)])
    w0 = backward(0, place, q_own, q_other, block, x, mean)
    warmth = summed_over_hours(w0) * scale
    return warmth, wetness, middle * scale


def solution(mesh):
    return jax.shard_map(
        per_device,
        mesh=mesh,
        in_specs=(
            P(("tm", "grid"), None),
            P(("tm", "grid"), None),
            P(None, "tm"),
            P(None, "grid"),
            P("grid", None),
            P("grid", None),
        ),
        out_specs=(P("tm", "grid"), P("tm", "grid"), P()),
        check_vma=False,
    )
```

```python
import functools

import jax
import jax.numpy as jnp
from jax import lax
from jax.experimental import pallas as pl
from jax.experimental.pallas import tpu as pltpu
from jax.sharding import PartitionSpec as P


BLK = 256
NCHUNK = 512
Y, Z, C = 4, 4, 2
F32, BF16 = jnp.float32, jnp.bfloat16
HIGHEST = lax.Precision.HIGHEST
MIB = 1 << 20


def thirds(v):
    high = v.astype(BF16)
    v = v - high.astype(F32)
    middle = v.astype(BF16)
    return high, middle, (v - middle.astype(F32)).astype(BF16)


def prepare_kernel(x0_ref, x1_ref, fading_ref, out_ref, block_ref, since_ref, to_end_ref, sems):
    n, _, _, width = out_ref.shape

    def copies():
        for i in range(n):
            for f, x_ref in enumerate((x0_ref, x1_ref)):
                yield pltpu.make_async_copy(x_ref.at[:, pl.ds(i * width, width)], out_ref.at[i, f], sems.at[2 * i + f])

    for copy in copies():
        copy.start()
    nb = fading_ref.shape[1] // BLK
    a = jnp.concatenate([fading_ref[f : f + 1, b * BLK : (b + 1) * BLK] for f in range(2) for b in range(nb)])
    log_a = jnp.log(a)
    r = lax.broadcasted_iota(jnp.int32, (BLK, BLK), 0)
    c = lax.broadcasted_iota(jnp.int32, (BLK, BLK), 1)
    upto = jnp.where(r <= c, 1.0, 0.0)
    inclusive = jnp.dot(log_a, upto, precision=HIGHEST, preferred_element_type=F32)
    exclusive = jnp.where(lax.broadcasted_iota(jnp.int32, a.shape, 1) == 0, 0.0, pltpu.roll(inclusive, 1, 1))
    column = exclusive.T
    fresh = 1.0 - a
    total = inclusive[:, BLK - 1 : BLK]
    ends = []
    for f in range(2):
        sums = [total[f * nb + b : f * nb + b + 1] for b in range(nb)]
        ahead = jnp.zeros_like(sums[0])
        for b in range(nb):
            k = f * nb + b
            row = slice(k, k + 1)
            weight = jnp.exp(jnp.minimum(column[:, k : k + 1] - inclusive[row], 0.0)) * fresh[row]
            block_ref[k, :BLK, :BLK] = jnp.where(r == c, 1.0, jnp.where(c < r, -weight, 0.0))
            block_ref[k, :BLK, BLK:] = jnp.broadcast_to(jnp.exp(column[:, k : k + 1]), (BLK, 128))
            last = jnp.exp(sums[b] - inclusive[row]) * fresh[row]
            block_ref[k, BLK:, :BLK] = jnp.broadcast_to(last, (8, BLK))
            block_ref[k, BLK:, BLK:] = jnp.broadcast_to(-jnp.exp(sums[b]), (8, 128))
            behind = sum(sums[b + 1 :], jnp.zeros_like(ahead))
            since_ref[row] = jnp.exp(ahead + exclusive[row])
            ends.append(jnp.exp(behind + (sums[b] - inclusive[row])) * fresh[row])
            ahead = ahead + sums[b]
    to_end_ref[...] = jnp.concatenate(ends).T
    for copy in copies():
        copy.wait()


def prepare(x0, x1, fading, n):
    rows, points = x0.shape
    width = points // n
    count = fading.size // BLK
    whole = pl.BlockSpec(memory_space=pltpu.VMEM)
    return pl.pallas_call(
        prepare_kernel,
        in_specs=[pl.BlockSpec(memory_space=pl.ANY), pl.BlockSpec(memory_space=pl.ANY), whole],
        out_specs=[pl.BlockSpec(memory_space=pl.ANY), whole, whole, whole],
        out_shape=[
            jax.ShapeDtypeStruct((n, 2, rows, width), x0.dtype),
            jax.ShapeDtypeStruct((count, BLK + 8, BLK + 128), F32),
            jax.ShapeDtypeStruct((count, BLK), F32),
            jax.ShapeDtypeStruct((BLK, count), F32),
        ],
        scratch_shapes=[pltpu.SemaphoreType.DMA((2 * n,))],
        compiler_params=pltpu.CompilerParams(vmem_limit_bytes=24 * MIB),
        cost_estimate=pl.CostEstimate(flops=0, bytes_accessed=8 * x0.size, transcendentals=0),
        name="prepare",
    )(x0, x1, fading)


def forward_kernel(
    field, place_ref, x_ref, op_ref, block_ref, to_end_ref, start_ref, own_ref, other_ref, end_ref, begin_ref, y_ref, s_ref
):
    step = pl.program_id(0)
    _, _, rows, chunk = x_ref.shape
    hours, rank = y_ref.shape
    nb = hours // BLK
    x = x_ref[:, 0].reshape(hours, chunk)
    y = jnp.dot(x, op_ref[...], preferred_element_type=F32)
    start = jnp.concatenate([part.astype(F32) for part in thirds(start_ref[field : field + 1])] + [jnp.zeros((5, chunk), F32)])
    begin = jnp.dot(start.astype(BF16), op_ref[...], preferred_element_type=F32)

    @pl.when(step == 0)
    def _():
        y_ref[...] = y
        s_ref[...] = begin

    @pl.when(step > 0)
    def _():
        y_ref[...] += y
        s_ref[...] += begin

    end = jnp.zeros((1, chunk), F32)
    for b in range(nb):
        part = x_ref[b * (BLK // rows) : (b + 1) * (BLK // rows), 0].reshape(BLK, chunk).astype(F32)
        k = field * nb + b
        end = end + (part * to_end_ref[:, k : k + 1]).sum(axis=0, keepdims=True)
    last = pl.num_programs(0) - 1
    for i in range(begin_ref.shape[1] // chunk):

        @pl.when(step == i)
        def _():
            end_ref[0:1, i * chunk : (i + 1) * chunk] = end
            begin_ref[:, i * chunk : (i + 1) * chunk] = start_ref[field : field + 1]

    @pl.when(step == last)
    def _():
        width = begin_ref.shape[1] - rank
        state = jnp.zeros((1, rank), F32)
        gain = jnp.ones((1, 1), F32)
        per = BLK // rows
        for b in range(nb):
            block = block_ref[b]
            out = jnp.dot(block[:, :BLK], y_ref[b * BLK : (b + 1) * BLK], precision=HIGHEST, preferred_element_type=F32)
            out = out - block[:, BLK : BLK + 1] * state
            part = out[:BLK].reshape(per, rows, rank)
            half, at = divmod(b, nb // 2)

            @pl.when(place_ref[0] == half)
            def _():
                own_ref[at * per : (at + 1) * per] = part

            @pl.when(place_ref[0] != half)
            def _():
                other_ref[at * per : (at + 1) * per] = part

            state = out[BLK : BLK + 1]
            gain = gain * -block[BLK : BLK + 1, BLK : BLK + 1]
        end_ref[0:1, width:] = state
        end_ref[1:2] = jnp.broadcast_to(gain, (1, width + rank))
        begin_ref[:, width:] = s_ref[0:1] + s_ref[1:2] + s_ref[2:3]


def forward(field, place, x, operator, tables, starting):
    block, _, to_end = tables
    n, _, rows, width = x.shape
    rank = operator.shape[1]
    hours, chunk = n * rows, 2 * NCHUNK
    nb = hours // BLK
    half = jax.ShapeDtypeStruct((n // 2, rows, rank), F32)
    fixed = lambda *shape: pl.BlockSpec(shape, lambda i: (0,) * len(shape))
    return pl.pallas_call(
        functools.partial(forward_kernel, field),
        grid=(width // chunk,),
        in_specs=[
            pl.BlockSpec(memory_space=pltpu.SMEM),
            pl.BlockSpec((n, 1, rows, chunk), lambda i: (0, field, 0, i)),
            pl.BlockSpec((chunk, rank), lambda i: (i, 0)),
            pl.BlockSpec((nb, BLK + 8, BLK + 128), lambda i: (field, 0, 0)),
            fixed(BLK, 2 * nb),
            pl.BlockSpec((2, chunk), lambda i: (0, i)),
        ],
        out_specs=[fixed(n // 2, rows, rank), fixed(n // 2, rows, rank), fixed(2, width + rank), fixed(1, width + rank)],
        out_shape=[half, half, jax.ShapeDtypeStruct((2, width + rank), F32), jax.ShapeDtypeStruct((1, width + rank), F32)],
        scratch_shapes=[pltpu.VMEM((hours, rank), F32), pltpu.VMEM((8, rank), F32)],
        compiler_params=pltpu.CompilerParams(vmem_limit_bytes=54 * MIB),
        cost_estimate=pl.CostEstimate(
            flops=2 * hours * width * rank, bytes_accessed=2 * hours * width, transcendentals=0
        ),
        name="forward",
    )(place, x, operator, block, to_end, starting)


def backward_kernel(
    place_ref, own_ref, other_ref, block_ref, x_ref, enter_ref, send0_ref, keep0_ref, send1_ref, keep1_ref, z_ref, carried
):
    step = pl.program_id(0)
    rank = own_ref.shape[2]
    quarter = rank // 4

    @pl.when(step == 0)
    def _():
        nb = block_ref.shape[0]
        rows = own_ref.shape[1]
        per = BLK // rows
        swap = place_ref[1]
        reverse = jnp.zeros((rank, 1), F32)

        def placed(ref, value, cols, base=0):
            for d in range(4):
                at = pl.multiple_of(base + jnp.bitwise_xor(d, swap) * quarter, quarter)
                ref[pl.ds(at, quarter), cols] = value[d * quarter : (d + 1) * quarter]

        for b in reversed(range(nb)):
            half, at = divmod(b, nb // 2)
            own = own_ref[at * per : (at + 1) * per].reshape(BLK, rank)
            other = other_ref[at * per : (at + 1) * per].reshape(BLK, rank)
            q = jnp.where(place_ref[0] == half, own.astype(F32), other.astype(F32)).T.astype(BF16)
            out = jnp.zeros((rank, BLK + 128), F32)
            for part in reversed(thirds(block_ref[b, :BLK])):
                out = out + jnp.dot(q, part, preferred_element_type=F32)
            out = out - reverse * block_ref[b, BLK : BLK + 1, :]
            z = out[:, :BLK]
            high = z.astype(BF16)
            cols = slice(b * BLK, (b + 1) * BLK)
            placed(z_ref, high, cols)
            placed(z_ref, (z - high.astype(F32)).astype(BF16), cols, rank)
            reverse = out[:, BLK : BLK + 1]
        placed(carried, jnp.broadcast_to(reverse, carried.shape), slice(0, carried.shape[1]))

    x = x_ref[:, 0].reshape(z_ref.shape[1], x_ref.shape[3])
    w = jnp.dot(z_ref[...], x, preferred_element_type=F32)
    w = w[:rank] + w[rank:] - carried[:, 0:1] * enter_ref[...]
    w = [w[k * quarter : (k + 1) * quarter].astype(BF16) for k in range(4)]

    @pl.when(step < pl.num_programs(0) // 2)
    def _():
        send0_ref[:quarter], send0_ref[quarter:] = w[1], w[2]
        keep0_ref[:quarter], keep0_ref[quarter:] = w[0], w[3]

    @pl.when(step >= pl.num_programs(0) // 2)
    def _():
        send1_ref[:quarter], send1_ref[quarter:] = w[2], w[3]
        keep1_ref[:quarter], keep1_ref[quarter:] = w[0], w[1]


def backward(f, place, own, other, block, x, enter):
    n, _, rows, width = x.shape
    hours, rank = n * rows, own.shape[2]
    nb = hours // BLK
    steps = width // NCHUNK // 2
    q_spec = pl.BlockSpec((n // 2, rows, rank), lambda i: (0, 0, 0))
    left = pl.BlockSpec((rank // 2, NCHUNK), lambda i: (0, jnp.minimum(i, steps - 1)))
    right = pl.BlockSpec((rank // 2, NCHUNK), lambda i: (0, jnp.maximum(i - steps, 0)))
    piece = jax.ShapeDtypeStruct((rank // 2, width // 2), BF16)
    return pl.pallas_call(
        backward_kernel,
        grid=(2 * steps,),
        in_specs=[
            pl.BlockSpec(memory_space=pltpu.SMEM),
            q_spec,
            q_spec,
            pl.BlockSpec((nb, BLK + 8, BLK + 128), lambda i: (f, 0, 0)),
            pl.BlockSpec((n, 1, rows, NCHUNK), lambda i: (0, f, 0, i)),
            pl.BlockSpec((1, NCHUNK), lambda i: (0, i)),
        ],
        out_specs=[left, left, right, right],
        out_shape=[piece] * 4,
        scratch_shapes=[
            pltpu.VMEM((2 * rank, hours), BF16),
            pltpu.VMEM((rank, 128), F32),
        ],
        compiler_params=pltpu.CompilerParams(vmem_limit_bytes=54 * MIB),
        cost_estimate=pl.CostEstimate(
            flops=4 * hours * width * rank, bytes_accessed=2 * hours * width, transcendentals=0
        ),
        name="backward",
    )(place, own, other, block, x, enter)


def cross_kernel(own0_ref, other0_ref, own1_ref, other1_ref, out_ref):
    n, rows, rank = own0_ref.shape
    out = jnp.zeros(out_ref.shape, F32)
    for ref0, ref1 in ((own0_ref, own1_ref), (other0_ref, other1_ref)):
        left = ref0[...].reshape(n * rows, rank).astype(F32).T.astype(BF16)
        out = out + jnp.dot(left, ref1[...].reshape(n * rows, rank), preferred_element_type=F32)
    out_ref[...] = out.astype(out_ref.dtype)


def cross(q0, q1):
    rank, size = q0[0].shape[2], q0[0].size
    whole = pl.BlockSpec(memory_space=pltpu.VMEM)
    return pl.pallas_call(
        cross_kernel,
        out_shape=jax.ShapeDtypeStruct((rank, rank), BF16),
        in_specs=[whole] * 4,
        out_specs=whole,
        compiler_params=pltpu.CompilerParams(vmem_limit_bytes=8 * MIB),
        cost_estimate=pl.CostEstimate(flops=4 * size * rank, bytes_accessed=8 * size, transcendentals=0),
        name="cross",
    )(*q0, *q1)


def all_to_all(x, axis, groups=None):
    return lax.all_to_all(x, axis, split_axis=0, concat_axis=0, tiled=True, axis_index_groups=groups)


def shifted(x, by):
    n = lax.axis_size("tm")
    return lax.ppermute(x, "tm", [(i, (i + by) % n) for i in range(n)])


def paired(x, by):
    return lax.ppermute(x, "tm", [(i, i ^ by) for i in range(lax.axis_size("tm"))])


def across(x):
    return lax.ppermute(x, "grid", [(g, g ^ 1) for g in range(Y * Z * C)])


def entering(end, start, i):
    total, so_far = jnp.zeros_like(start), jnp.ones_like(start)
    for d in range(1, lax.axis_size("tm")):
        got = shifted(end, d)
        total = total + jnp.where(i >= d, so_far * got[:1], 0.0)
        so_far = so_far * jnp.where(i >= d, got[1:], 1.0)
    return total + so_far * start


def summed_over_hours(pieces):
    send0, keep0, send1, keep1 = pieces
    q = send0.shape[0] // 2
    wide = lambda v: v.astype(F32)
    got0 = paired(send0, 1)
    got1 = paired(send1, 3)
    last0 = paired((wide(keep0[q:]) + wide(got0[q:])).astype(BF16), 3)
    last1 = paired((wide(keep1[q:]) + wide(got1[:q])).astype(BF16), 1)
    left = wide(keep0[:q]) + wide(got0[:q]) + wide(last0)
    right = wide(keep1[:q]) + wide(got1[q:]) + wide(last1)
    return jnp.concatenate([left, right], axis=1)


def per_device(x0, x1, fading, starting, operator0, operator1):
    grid = lax.axis_size("grid")
    rows, points = x0.shape
    width, hours = points // grid, rows * grid
    scale = (hours * lax.axis_size("tm")) ** -0.5
    core, shard = lax.axis_index("grid") & (C - 1), lax.axis_index("tm")
    place = jnp.stack([core, shard]).astype(jnp.int32)
    n = grid // C
    groups = [[k * C + c for k in range(n)] for c in range(C)]
    barrier = lax.optimization_barrier

    def lead(f, x, core, shard):
        own, other, end, start = forward(f, place, x, operators[f], tables, starting)
        enter = entering(end, start, shard)
        mean, part = enter[:, :width], enter[:, width:]
        part = part + across(part)
        since = lax.dynamic_index_in_dim(tables[1].reshape(2, C, n, rows)[f], core, 0, keepdims=False)
        p = own + across(other) - since[..., None] * part[None]
        return p.astype(BF16), mean

    def there(p):
        return all_to_all(p, "grid", groups).astype(F32).sum(axis=0).astype(BF16)

    def back(q):
        own = all_to_all(jnp.broadcast_to(q, (n, *q.shape)), "grid", groups)
        return own, across(own)

    packed, *tables = prepare(x0, x1, fading, grid)
    packed, rest = barrier((packed, (tables, place, core, shard, starting, operator0, operator1)))
    x = all_to_all(packed, "grid")
    x, (tables, place, core, shard, starting, *operators) = barrier((x, rest))
    p0, mean0 = lead(0, x, core, shard)
    r0 = there(p0)
    p1, mean1 = lead(1, x, core, shard)
    q0 = back(r0)
    p1, q0 = barrier((p1, q0))
    r1 = there(p1)
    w1 = backward(1, place, *q0, tables[0], x, mean1)
    q1 = back(r1)
    wetness = summed_over_hours(w1) * scale
    w0 = backward(0, place, *q1, tables[0], x, mean0)
    warmth = summed_over_hours(w0) * scale
    sent = lax.dynamic_index_in_dim(cross(q0, q1).reshape(C, -1, operator0.shape[1]), core, 0, keepdims=False)
    half = sent.astype(F32)
    for d in range(1, lax.axis_size("tm")):
        half = half + shifted(sent, d).astype(F32)
    partner = across(half)
    middle = jnp.concatenate([jnp.where(core == 0, half, partner), jnp.where(core == 0, partner, half)])
    return warmth, wetness, middle * scale


def solution(mesh):
    return jax.shard_map(
        per_device,
        mesh=mesh,
        in_specs=(
            P(("tm", "grid"), None),
            P(("tm", "grid"), None),
            P(None, "tm"),
            P(None, "grid"),
            P("grid", None),
            P("grid", None),
        ),
        out_specs=(P("tm", "grid"), P("tm", "grid"), P()),
        check_vma=False,
    )
```

```python
import jax
import jax.numpy as jnp
from jax import lax
from jax.experimental import pallas as pl
from jax.experimental.pallas import tpu as pltpu
from jax.sharding import PartitionSpec as P


BLK = 256
NCHUNK = 768
TILE = 256
Y, Z, C = 4, 4, 2
F32, BF16 = jnp.float32, jnp.bfloat16
HIGHEST = lax.Precision.HIGHEST
MIB = 1 << 20


def thirds(v):
    high = v.astype(BF16)
    v = v - high.astype(F32)
    middle = v.astype(BF16)
    return high, middle, (v - middle.astype(F32)).astype(BF16)


def prepare_kernel(x0_ref, x1_ref, fading_ref, out_ref, block_ref, since_ref, to_end_ref, gain_ref, sems):
    n, _, _, width = out_ref.shape

    def copies():
        for i in range(n):
            for f, x_ref in enumerate((x0_ref, x1_ref)):
                yield pltpu.make_async_copy(x_ref.at[:, pl.ds(i * width, width)], out_ref.at[i, f], sems.at[2 * i + f])

    for copy in copies():
        copy.start()
    nb = fading_ref.shape[1] // BLK
    a = jnp.concatenate([fading_ref[f : f + 1, b * BLK : (b + 1) * BLK] for f in range(2) for b in range(nb)])
    log_a = jnp.log(a)
    r = lax.broadcasted_iota(jnp.int32, (BLK, BLK), 0)
    c = lax.broadcasted_iota(jnp.int32, (BLK, BLK), 1)
    upto = jnp.where(r <= c, 1.0, 0.0)
    inclusive = jnp.dot(log_a, upto, precision=HIGHEST, preferred_element_type=F32)
    exclusive = jnp.where(lax.broadcasted_iota(jnp.int32, a.shape, 1) == 0, 0.0, pltpu.roll(inclusive, 1, 1))
    column = exclusive.T
    fresh = 1.0 - a
    total = inclusive[:, BLK - 1 : BLK]
    for f in range(2):
        sums = [total[f * nb + b : f * nb + b + 1] for b in range(nb)]
        ahead = jnp.zeros_like(sums[0])
        for b in range(nb):
            k = f * nb + b
            row = slice(k, k + 1)
            weight = jnp.exp(jnp.minimum(column[:, k : k + 1] - inclusive[row], 0.0)) * fresh[row]
            block_ref[k, :BLK, :BLK] = jnp.where(r == c, 1.0, jnp.where(c < r, -weight, 0.0))
            block_ref[k, :BLK, BLK:] = jnp.broadcast_to(jnp.exp(column[:, k : k + 1]), (BLK, 128))
            last = jnp.exp(sums[b] - inclusive[row]) * fresh[row]
            block_ref[k, BLK:, :BLK] = jnp.broadcast_to(last, (8, BLK))
            block_ref[k, BLK:, BLK:] = jnp.broadcast_to(-jnp.exp(sums[b]), (8, 128))
            behind = sum(sums[b + 1 :], jnp.zeros_like(ahead))
            since_ref[row] = jnp.exp(ahead + exclusive[row])
            to_end_ref[row] = jnp.exp(behind + (sums[b] - inclusive[row])) * fresh[row]
            ahead = ahead + sums[b]
        gain_ref[f : f + 1] = jnp.broadcast_to(jnp.exp(ahead), (1, BLK))
    for copy in copies():
        copy.wait()


def prepare(x0, x1, fading, n):
    rows, points = x0.shape
    width = points // n
    count = fading.size // BLK
    whole = pl.BlockSpec(memory_space=pltpu.VMEM)
    return pl.pallas_call(
        prepare_kernel,
        in_specs=[pl.BlockSpec(memory_space=pl.ANY), pl.BlockSpec(memory_space=pl.ANY), whole],
        out_specs=[pl.BlockSpec(memory_space=pl.ANY), whole, whole, whole, whole],
        out_shape=[
            jax.ShapeDtypeStruct((n, 2, rows, width), x0.dtype),
            jax.ShapeDtypeStruct((count, BLK + 8, BLK + 128), F32),
            jax.ShapeDtypeStruct((count, BLK), F32),
            jax.ShapeDtypeStruct((count, BLK), F32),
            jax.ShapeDtypeStruct((2, BLK), F32),
        ],
        scratch_shapes=[pltpu.SemaphoreType.DMA((2 * n,))],
        compiler_params=pltpu.CompilerParams(vmem_limit_bytes=20 * MIB),
        cost_estimate=pl.CostEstimate(flops=0, bytes_accessed=8 * x0.size, transcendentals=0),
        name="prepare",
    )(x0, x1, fading)


def exact_dot(left, right):
    lh, lm, ll = thirds(left)
    rh, rm, rl = thirds(right)
    return jnp.dot(
        jnp.concatenate([ll, lm, lh, lm, lh, lh], axis=1),
        jnp.concatenate([rh, rm, rl, rh, rm, rh], axis=0),
        preferred_element_type=F32,
    )


def forward_kernel(
    place_ref, x_ref, op0_ref, op1_ref, block_ref, start_ref, p_ref, end_ref, begin_ref, y_ref
):
    f, step = pl.program_id(0), pl.program_id(1)
    count, _, rows, width = x_ref.shape
    hours, rank = y_ref.shape
    nb = hours // BLK
    at = pl.multiple_of(step * (count * rows), count * rows)

    def products(k, op_ref):
        y_ref[pl.ds(at, count * rows)] = jnp.dot(
            x_ref[:, 0].reshape(count * rows, width), op_ref[...], preferred_element_type=F32
        )

        @pl.when(step == 0)
        def _():
            parts = thirds(start_ref[k : k + 1])
            start = jnp.concatenate([part.astype(F32) for part in parts] + [jnp.zeros((5, width), F32)])
            begin = jnp.dot(start.astype(BF16), op_ref[...], preferred_element_type=F32)
            begin_ref[k : k + 1] = begin[0:1] + begin[1:2] + begin[2:3]

    for k, op_ref in enumerate((op0_ref, op1_ref)):

        @pl.when(f == k)
        def _():
            products(k, op_ref)

    @pl.when(step == pl.num_programs(1) - 1)
    def _():
        state = jnp.zeros((1, rank), F32)
        per = BLK // rows
        outs = [exact_dot(block_ref[b, :, :BLK], y_ref[b * BLK : (b + 1) * BLK]) for b in range(nb)]
        for b, out in enumerate(outs):
            out = out - block_ref[b, :, BLK : BLK + 1] * state
            half, at = divmod(b, nb // 2)
            slot = jnp.bitwise_xor(half, place_ref[0])
            p_ref[slot, at * per : (at + 1) * per, 0] = out[:BLK].reshape(per, rows, rank)
            state = out[BLK : BLK + 1]
        end_ref[pl.ds(f, 1)] = state


def forward(place, x, operators, block, starting):
    n, _, rows, width = x.shape
    rank = operators[0].shape[1]
    hours, steps = n * rows, 2
    nb = hours // BLK
    halves = jax.ShapeDtypeStruct((2, n // 2, 2, rows, rank), F32)
    halves_spec = pl.BlockSpec((2, n // 2, 1, rows, rank), lambda f, i: (0, 0, f, 0, 0))
    pair, pair_spec = jax.ShapeDtypeStruct((2, rank), F32), pl.BlockSpec((2, rank), lambda f, i: (0, 0))
    op_spec = pl.BlockSpec((width, rank), lambda f, i: (0, 0))
    return pl.pallas_call(
        forward_kernel,
        grid=(2, steps),
        in_specs=[
            pl.BlockSpec(memory_space=pltpu.SMEM),
            pl.BlockSpec((n // steps, 1, rows, width), lambda f, i: (i, f, 0, 0)),
            op_spec,
            op_spec,
            pl.BlockSpec((nb, BLK + 8, BLK + 128), lambda f, i: (f, 0, 0)),
            pl.BlockSpec((2, width), lambda f, i: (0, 0)),
        ],
        out_specs=[halves_spec, pair_spec, pair_spec],
        out_shape=[halves, pair, pair],
        scratch_shapes=[pltpu.VMEM((hours, rank), F32)],
        compiler_params=pltpu.CompilerParams(vmem_limit_bytes=24 * MIB),
        cost_estimate=pl.CostEstimate(
            flops=4 * hours * width * rank, bytes_accessed=4 * hours * width, transcendentals=0
        ),
        name="forward",
    )(place, x, *operators, block, starting)


def backward_kernel(place_ref, own_ref, other_ref, block_ref, x_ref, enter_ref, keep_ref, send_ref, z_ref, carried):
    step = pl.program_id(0)
    rank = own_ref.shape[3]
    quarter = rank // 4

    @pl.when(step == 0)
    def _():
        nb = block_ref.shape[0]
        rows = own_ref.shape[2]
        per = BLK // rows
        reverse = jnp.zeros((rank, 1), F32)

        def placed(ref, value, cols, base=0):
            for order in range(2):
                for d in range(4):
                    to = jnp.bitwise_xor(d, place_ref[1])
                    if order == 0:
                        to = jnp.where(to == 0, 0, to % 3 + 1)
                    at = pl.multiple_of(base + to * quarter, quarter)
                    ref[order, pl.ds(at, quarter), cols] = value[d * quarter : (d + 1) * quarter]

        parts = []
        for b in range(nb):
            half, at = divmod(b, nb // 2)
            own = own_ref[at * per : (at + 1) * per, 0].reshape(BLK, rank)
            other = other_ref[at * per : (at + 1) * per, 0].reshape(BLK, rank)
            q = jnp.where(place_ref[0] == half, own.astype(F32), other.astype(F32)).T.astype(BF16)
            high, middle, low = thirds(block_ref[b, :BLK])
            parts.append(
                jnp.dot(
                    jnp.concatenate([q, q, q], axis=1),
                    jnp.concatenate([low, middle, high], axis=0),
                    preferred_element_type=F32,
                )
            )
        for b in reversed(range(nb)):
            out = parts[b] - reverse * block_ref[b, BLK : BLK + 1, :]
            z = out[:, :BLK]
            high = z.astype(BF16)
            cols = slice(b * BLK, (b + 1) * BLK)
            placed(z_ref, high, cols)
            placed(z_ref, (z - high.astype(F32)).astype(BF16), cols, rank)
            reverse = out[:, BLK : BLK + 1]
        placed(carried, jnp.broadcast_to(reverse, carried.shape[1:]), slice(0, carried.shape[2]))

    hours = z_ref.shape[2]
    order = step // (pl.num_programs(0) // 2)
    for t in range(x_ref.shape[3] // TILE):
        cols = slice(t * TILE, (t + 1) * TILE)
        w = jnp.dot(z_ref[order], x_ref[:, 0, :, cols].reshape(hours, TILE), preferred_element_type=F32)
        w = w[:rank] + w[rank:] - carried[order][:, 0:1] * enter_ref[0, :, cols]
        w = w.astype(BF16)
        keep_ref[0, :, cols] = w[: rank // 2]
        send_ref[0, :, cols] = w[rank // 2 :]


def backward(f, place, own, other, block, x, enter):
    n, _, rows, width = x.shape
    hours, rank = n * rows, own.shape[3]
    nb = hours // BLK
    steps = width // NCHUNK // 2
    q_spec = pl.BlockSpec((n // 2, 1, rows, rank), lambda i: (0, 1 - f, 0, 0))
    out_spec = pl.BlockSpec((1, rank // 2, NCHUNK), lambda i: (i // steps, 0, i % steps))
    piece = jax.ShapeDtypeStruct((2, rank // 2, width // 2), BF16)
    return pl.pallas_call(
        backward_kernel,
        grid=(2 * steps,),
        in_specs=[
            pl.BlockSpec(memory_space=pltpu.SMEM),
            q_spec,
            q_spec,
            pl.BlockSpec((nb, BLK + 8, BLK + 128), lambda i: (f, 0, 0)),
            pl.BlockSpec((n, 1, rows, NCHUNK), lambda i: (0, f, 0, i)),
            pl.BlockSpec((1, 1, NCHUNK), lambda i: (f, 0, i)),
        ],
        out_specs=[out_spec, out_spec],
        out_shape=[piece, piece],
        scratch_shapes=[
            pltpu.VMEM((2, 2 * rank, hours), BF16),
            pltpu.VMEM((2, rank, 128), F32),
        ],
        compiler_params=pltpu.CompilerParams(vmem_limit_bytes=54 * MIB),
        cost_estimate=pl.CostEstimate(
            flops=4 * hours * width * rank, bytes_accessed=2 * hours * width, transcendentals=0
        ),
        name="backward",
    )(place, own, other, block, x, enter[:, None])


def cross_kernel(place_ref, own_ref, other_ref, out_ref):
    n, _, rows, rank = own_ref.shape
    out = jnp.zeros(out_ref.shape, F32)
    for ref in (own_ref, other_ref):
        left = ref[:, 0].reshape(n * rows, rank).astype(F32).T.astype(BF16)
        out = out + jnp.dot(left, ref[:, 1].reshape(n * rows, rank), preferred_element_type=F32)
    out_ref[...] = out


def cross(place, own, other):
    rank = own.shape[3]
    whole = pl.BlockSpec(memory_space=pltpu.VMEM)
    return pl.pallas_call(
        cross_kernel,
        out_shape=jax.ShapeDtypeStruct((rank, rank), F32),
        in_specs=[pl.BlockSpec(memory_space=pltpu.SMEM), whole, whole],
        out_specs=whole,
        compiler_params=pltpu.CompilerParams(vmem_limit_bytes=8 * MIB),
        cost_estimate=pl.CostEstimate(flops=2 * own.size * rank, bytes_accessed=4 * own.size, transcendentals=0),
        name="cross",
    )(place, own, other)


def all_to_all(x, axis, groups=None):
    return lax.all_to_all(x, axis, split_axis=0, concat_axis=0, tiled=True, axis_index_groups=groups)


def shifted(x, by):
    n = lax.axis_size("tm")
    return lax.ppermute(x, "tm", [(i, (i + by) % n) for i in range(n)])


def paired(x, by):
    return lax.ppermute(x, "tm", [(i, i ^ by) for i in range(lax.axis_size("tm"))])


def across(x):
    return lax.ppermute(x, "grid", [(g, g ^ 1) for g in range(Y * Z * C)])


def entering(end, gain, start, i):
    message = jnp.concatenate([end, jnp.broadcast_to(gain, end.shape)])
    total, so_far = jnp.zeros_like(end), jnp.ones_like(end)
    for d in range(1, lax.axis_size("tm")):
        got = shifted(message, d)
        total = total + jnp.where(i >= d, so_far * got[:2], 0.0)
        so_far = so_far * jnp.where(i >= d, got[2:4], 1.0)
    return total + so_far * start


def summed_over_hours(pieces):
    (keep0, keep1), (send0, send1) = pieces
    q = send0.shape[0] // 2
    wide = lambda v: v.astype(F32)
    got0 = paired(send0, 1)
    got1 = paired(send1, 3)
    last0 = paired((wide(keep0[q:]) + wide(got0[q:])).astype(BF16), 3)
    last1 = paired((wide(keep1[q:]) + wide(got1[:q])).astype(BF16), 1)
    left = wide(keep0[:q]) + wide(got0[:q]) + wide(last0)
    right = wide(keep1[:q]) + wide(got1[q:]) + wide(last1)
    return jnp.concatenate([left, right], axis=1)


def per_device(x0, x1, fading, starting, operator0, operator1):
    grid = lax.axis_size("grid")
    rows, _ = x0.shape
    hours = rows * grid
    scale = (hours * lax.axis_size("tm")) ** -0.5
    core, shard = lax.axis_index("grid") & (C - 1), lax.axis_index("tm")
    place = jnp.stack([core, shard]).astype(jnp.int32)
    n = grid // C
    groups = [[k * C + c for k in range(n)] for c in range(C)]
    packed, *tables = prepare(x0, x1, fading, grid)
    rest = (tables, operator0, operator1, place, core, shard, starting)
    packed, rest = lax.optimization_barrier((packed, rest))
    x = all_to_all(packed, "grid")
    x, (tables, *operators, place, core, shard, starting) = lax.optimization_barrier((x, rest))
    block, since, to_end, gain = tables
    (own, other), end, begin = forward(place, x, operators, block, starting)
    enter = entering(end, gain[:, :1], begin, shard)
    enter = enter + across(enter)
    since = lax.dynamic_index_in_dim(since.reshape(2, C, n, rows), core, 1, keepdims=False).transpose(1, 0, 2)
    p = own + across(other) - since[..., None] * enter[None, :, None]
    p, x = lax.optimization_barrier((p.astype(BF16), x))
    p = all_to_all(p, "grid", groups)
    q = p.astype(F32).sum(axis=0).astype(BF16)
    q_own = all_to_all(jnp.broadcast_to(q, p.shape), "grid", groups)
    q_other = across(q_own)
    weight = to_end.reshape(2, grid, rows).transpose(1, 0, 2)[..., None]
    mean = entering((x.astype(F32) * weight).sum(axis=(0, 2)), gain[:, :1], starting, shard)
    w1 = backward(1, place, q_own, q_other, block, x, mean)
    wetness = summed_over_hours(w1) * scale
    sent = lax.dynamic_index_in_dim(cross(place, q_own, q_other).reshape(C, -1, q.shape[2]), core, 0, keepdims=False)
    sent = sent.astype(BF16)
    half = sent.astype(F32)
    for d in range(1, lax.axis_size("tm")):
        half = half + shifted(sent, d).astype(F32)
    partner = across(half)
    middle = jnp.concatenate([jnp.where(core == 0, half, partner), jnp.where(core == 0, partner, half)])
    w0 = backward(0, place, q_own, q_other, block, x, mean)
    warmth = summed_over_hours(w0) * scale
    return warmth, wetness, middle * scale


def solution(mesh):
    return jax.shard_map(
        per_device,
        mesh=mesh,
        in_specs=(
            P(("tm", "grid"), None),
            P(("tm", "grid"), None),
            P(None, "tm"),
            P(None, "grid"),
            P("grid", None),
            P("grid", None),
        ),
        out_specs=(P("tm", "grid"), P("tm", "grid"), P()),
        check_vma=False,
    )
```

```python
import jax
import jax.numpy as jnp
from jax import lax
from jax.experimental import pallas as pl
from jax.experimental.pallas import tpu as pltpu
from jax.sharding import PartitionSpec as P


BLK = 256
NCHUNK = 768
TILE = 256
Y, Z, C = 4, 4, 2
F32, BF16 = jnp.float32, jnp.bfloat16
HIGHEST = lax.Precision.HIGHEST
MIB = 1 << 20


def thirds(v):
    high = v.astype(BF16)
    v = v - high.astype(F32)
    middle = v.astype(BF16)
    return high, middle, (v - middle.astype(F32)).astype(BF16)


def prepare_kernel(x0_ref, x1_ref, fading_ref, out_ref, block_ref, since_ref, to_end_ref, gain_ref, sems):
    n, _, _, width = out_ref.shape

    def copies():
        for i in range(n):
            for f, x_ref in enumerate((x0_ref, x1_ref)):
                yield pltpu.make_async_copy(x_ref.at[:, pl.ds(i * width, width)], out_ref.at[i, f], sems.at[2 * i + f])

    for copy in copies():
        copy.start()
    nb = fading_ref.shape[1] // BLK
    a = jnp.concatenate([fading_ref[f : f + 1, b * BLK : (b + 1) * BLK] for f in range(2) for b in range(nb)])
    log_a = jnp.log(a)
    r = lax.broadcasted_iota(jnp.int32, (BLK, BLK), 0)
    c = lax.broadcasted_iota(jnp.int32, (BLK, BLK), 1)
    upto = jnp.where(r <= c, 1.0, 0.0)
    inclusive = jnp.dot(log_a, upto, precision=HIGHEST, preferred_element_type=F32)
    exclusive = jnp.where(lax.broadcasted_iota(jnp.int32, a.shape, 1) == 0, 0.0, pltpu.roll(inclusive, 1, 1))
    column = exclusive.T
    fresh = 1.0 - a
    total = inclusive[:, BLK - 1 : BLK]
    for f in range(2):
        sums = [total[f * nb + b : f * nb + b + 1] for b in range(nb)]
        ahead = jnp.zeros_like(sums[0])
        for b in range(nb):
            k = f * nb + b
            row = slice(k, k + 1)
            weight = jnp.exp(jnp.minimum(column[:, k : k + 1] - inclusive[row], 0.0)) * fresh[row]
            block_ref[k, :BLK, :BLK] = jnp.where(r == c, 1.0, jnp.where(c < r, -weight, 0.0))
            block_ref[k, :BLK, BLK:] = jnp.broadcast_to(jnp.exp(column[:, k : k + 1]), (BLK, 128))
            last = jnp.exp(sums[b] - inclusive[row]) * fresh[row]
            block_ref[k, BLK:, :BLK] = jnp.broadcast_to(last, (8, BLK))
            block_ref[k, BLK:, BLK:] = jnp.broadcast_to(-jnp.exp(sums[b]), (8, 128))
            behind = sum(sums[b + 1 :], jnp.zeros_like(ahead))
            since_ref[row] = jnp.exp(ahead + exclusive[row])
            to_end_ref[row] = jnp.exp(behind + (sums[b] - inclusive[row])) * fresh[row]
            ahead = ahead + sums[b]
        gain_ref[f : f + 1] = jnp.broadcast_to(jnp.exp(ahead), (1, BLK))
    for copy in copies():
        copy.wait()


def prepare(x0, x1, fading, n):
    rows, points = x0.shape
    width = points // n
    count = fading.size // BLK
    whole = pl.BlockSpec(memory_space=pltpu.VMEM)
    return pl.pallas_call(
        prepare_kernel,
        in_specs=[pl.BlockSpec(memory_space=pl.ANY), pl.BlockSpec(memory_space=pl.ANY), whole],
        out_specs=[pl.BlockSpec(memory_space=pl.ANY), whole, whole, whole, whole],
        out_shape=[
            jax.ShapeDtypeStruct((n, 2, rows, width), x0.dtype),
            jax.ShapeDtypeStruct((count, BLK + 8, BLK + 128), F32),
            jax.ShapeDtypeStruct((count, BLK), F32),
            jax.ShapeDtypeStruct((count, BLK), F32),
            jax.ShapeDtypeStruct((2, BLK), F32),
        ],
        scratch_shapes=[pltpu.SemaphoreType.DMA((2 * n,))],
        compiler_params=pltpu.CompilerParams(vmem_limit_bytes=20 * MIB),
        cost_estimate=pl.CostEstimate(flops=0, bytes_accessed=8 * x0.size, transcendentals=0),
        name="prepare",
    )(x0, x1, fading)


def exact_dot(left, right):
    lh, lm, ll = thirds(left)
    rh, rm, rl = thirds(right)
    return jnp.dot(
        jnp.concatenate([ll, lm, lh, lm, lh, lh], axis=1),
        jnp.concatenate([rh, rm, rl, rh, rm, rh], axis=0),
        preferred_element_type=F32,
    )


def forward_kernel(
    place_ref, x_ref, op0_ref, op1_ref, block_ref, start_ref, own_ref, other_ref, end_ref, begin_ref, y_ref, p_ref
):
    f, step = pl.program_id(0), pl.program_id(1)
    count, _, rows, width = x_ref.shape
    hours, rank = y_ref.shape
    nb = hours // BLK
    at = pl.multiple_of(step * (count * rows), count * rows)

    def products(k, op_ref):
        y_ref[pl.ds(at, count * rows)] = jnp.dot(
            x_ref[:, 0].reshape(count * rows, width), op_ref[...], preferred_element_type=F32
        )

        @pl.when(step == 0)
        def _():
            parts = thirds(start_ref[k : k + 1])
            start = jnp.concatenate([part.astype(F32) for part in parts] + [jnp.zeros((5, width), F32)])
            begin = jnp.dot(start.astype(BF16), op_ref[...], preferred_element_type=F32)
            begin_ref[k : k + 1] = begin[0:1] + begin[1:2] + begin[2:3]

    for k, op_ref in enumerate((op0_ref, op1_ref)):

        @pl.when(f == k)
        def _():
            products(k, op_ref)

    @pl.when(step == pl.num_programs(1) - 1)
    def _():
        state = jnp.zeros((1, rank), F32)
        per = BLK // rows
        outs = [exact_dot(block_ref[b, :, :BLK], y_ref[b * BLK : (b + 1) * BLK]) for b in range(nb)]
        for b, out in enumerate(outs):
            out = out - block_ref[b, :, BLK : BLK + 1] * state
            half, at = divmod(b, nb // 2)
            p_ref[half, at * per : (at + 1) * per] = out[:BLK].reshape(per, rows, rank)
            state = out[BLK : BLK + 1]
        end_ref[pl.ds(f, 1)] = state
        own_ref[:, 0] = p_ref[place_ref[0]]
        other_ref[:, 0] = p_ref[1 - place_ref[0]]


def forward(place, x, operators, block, starting):
    n, _, rows, width = x.shape
    rank = operators[0].shape[1]
    hours, steps = n * rows, 2
    nb = hours // BLK
    half = jax.ShapeDtypeStruct((n // 2, 2, rows, rank), F32)
    half_spec = pl.BlockSpec((n // 2, 1, rows, rank), lambda f, i: (0, f, 0, 0))
    pair, pair_spec = jax.ShapeDtypeStruct((2, rank), F32), pl.BlockSpec((2, rank), lambda f, i: (0, 0))
    op_spec = pl.BlockSpec((width, rank), lambda f, i: (0, 0))
    return pl.pallas_call(
        forward_kernel,
        grid=(2, steps),
        in_specs=[
            pl.BlockSpec(memory_space=pltpu.SMEM),
            pl.BlockSpec((n // steps, 1, rows, width), lambda f, i: (i, f, 0, 0)),
            op_spec,
            op_spec,
            pl.BlockSpec((nb, BLK + 8, BLK + 128), lambda f, i: (f, 0, 0)),
            pl.BlockSpec((2, width), lambda f, i: (0, 0)),
        ],
        out_specs=[half_spec, half_spec, pair_spec, pair_spec],
        out_shape=[half, half, pair, pair],
        scratch_shapes=[pltpu.VMEM((hours, rank), F32), pltpu.VMEM((2, n // 2, rows, rank), F32)],
        compiler_params=pltpu.CompilerParams(vmem_limit_bytes=24 * MIB),
        cost_estimate=pl.CostEstimate(
            flops=4 * hours * width * rank, bytes_accessed=4 * hours * width, transcendentals=0
        ),
        name="forward",
    )(place, x, *operators, block, starting)


def backward_kernel(
    place_ref, own_ref, other_ref, block_ref, x_ref, enter_ref, keep0_ref, send0_ref, keep1_ref, send1_ref, z_ref, carried, w_ref
):
    step = pl.program_id(0)
    rank = own_ref.shape[3]
    quarter = rank // 4

    @pl.when(step == 0)
    def _():
        nb = block_ref.shape[0]
        rows = own_ref.shape[2]
        per = BLK // rows
        reverse = jnp.zeros((rank, 1), F32)

        def placed(ref, value, cols, base=0):
            for order in range(2):
                for d in range(4):
                    to = jnp.bitwise_xor(d, place_ref[1])
                    if order == 0:
                        to = jnp.where(to == 0, 0, to % 3 + 1)
                    at = pl.multiple_of(base + to * quarter, quarter)
                    ref[order, pl.ds(at, quarter), cols] = value[d * quarter : (d + 1) * quarter]

        parts = []
        for b in range(nb):
            half, at = divmod(b, nb // 2)
            own = own_ref[at * per : (at + 1) * per, 0].reshape(BLK, rank)
            other = other_ref[at * per : (at + 1) * per, 0].reshape(BLK, rank)
            q = jnp.where(place_ref[0] == half, own.astype(F32), other.astype(F32)).T.astype(BF16)
            high, middle, low = thirds(block_ref[b, :BLK])
            parts.append(
                jnp.dot(
                    jnp.concatenate([q, q, q], axis=1),
                    jnp.concatenate([low, middle, high], axis=0),
                    preferred_element_type=F32,
                )
            )
        for b in reversed(range(nb)):
            out = parts[b] - reverse * block_ref[b, BLK : BLK + 1, :]
            z = out[:, :BLK]
            high = z.astype(BF16)
            cols = slice(b * BLK, (b + 1) * BLK)
            placed(z_ref, high, cols)
            placed(z_ref, (z - high.astype(F32)).astype(BF16), cols, rank)
            reverse = out[:, BLK : BLK + 1]
        placed(carried, jnp.broadcast_to(reverse, carried.shape[1:]), slice(0, carried.shape[2]))

    hours = z_ref.shape[2]
    order = step // (pl.num_programs(0) // 2)
    for t in range(x_ref.shape[3] // TILE):
        cols = slice(t * TILE, (t + 1) * TILE)
        w = jnp.dot(z_ref[order], x_ref[:, 0, :, cols].reshape(hours, TILE), preferred_element_type=F32)
        w = w[:rank] + w[rank:] - carried[order][:, 0:1] * enter_ref[0, :, cols]
        w_ref[:, cols] = w.astype(BF16)
    for k, (keep_ref, send_ref) in enumerate(((keep0_ref, send0_ref), (keep1_ref, send1_ref))):

        @pl.when(order == k)
        def _():
            keep_ref[...] = w_ref[: rank // 2]
            send_ref[...] = w_ref[rank // 2 :]


def backward(f, place, own, other, block, x, enter):
    n, _, rows, width = x.shape
    hours, rank = n * rows, own.shape[3]
    nb = hours // BLK
    steps = width // NCHUNK // 2
    q_spec = pl.BlockSpec((n // 2, 1, rows, rank), lambda i: (0, 1 - f, 0, 0))
    left = pl.BlockSpec((rank // 2, NCHUNK), lambda i: (0, jnp.minimum(i, steps - 1)))
    right = pl.BlockSpec((rank // 2, NCHUNK), lambda i: (0, jnp.maximum(i - steps, 0)))
    piece = jax.ShapeDtypeStruct((rank // 2, width // 2), BF16)
    return pl.pallas_call(
        backward_kernel,
        grid=(2 * steps,),
        in_specs=[
            pl.BlockSpec(memory_space=pltpu.SMEM),
            q_spec,
            q_spec,
            pl.BlockSpec((nb, BLK + 8, BLK + 128), lambda i: (f, 0, 0)),
            pl.BlockSpec((n, 1, rows, NCHUNK), lambda i: (0, f, 0, i)),
            pl.BlockSpec((1, 1, NCHUNK), lambda i: (f, 0, i)),
        ],
        out_specs=[left, left, right, right],
        out_shape=[piece] * 4,
        scratch_shapes=[
            pltpu.VMEM((2, 2 * rank, hours), BF16),
            pltpu.VMEM((2, rank, 128), F32),
            pltpu.VMEM((rank, NCHUNK), BF16),
        ],
        compiler_params=pltpu.CompilerParams(vmem_limit_bytes=54 * MIB),
        cost_estimate=pl.CostEstimate(
            flops=4 * hours * width * rank, bytes_accessed=2 * hours * width, transcendentals=0
        ),
        name="backward",
    )(place, own, other, block, x, enter[:, None])


def cross_kernel(place_ref, own_ref, other_ref, out_ref):
    n, _, rows, rank = own_ref.shape
    out = jnp.zeros(out_ref.shape, F32)
    for ref in (own_ref, other_ref):
        left = ref[:, 0].reshape(n * rows, rank).astype(F32).T.astype(BF16)
        out = out + jnp.dot(left, ref[:, 1].reshape(n * rows, rank), preferred_element_type=F32)
    out_ref[...] = out


def cross(place, own, other):
    rank = own.shape[3]
    whole = pl.BlockSpec(memory_space=pltpu.VMEM)
    return pl.pallas_call(
        cross_kernel,
        out_shape=jax.ShapeDtypeStruct((rank, rank), F32),
        in_specs=[pl.BlockSpec(memory_space=pltpu.SMEM), whole, whole],
        out_specs=whole,
        compiler_params=pltpu.CompilerParams(vmem_limit_bytes=8 * MIB),
        cost_estimate=pl.CostEstimate(flops=2 * own.size * rank, bytes_accessed=4 * own.size, transcendentals=0),
        name="cross",
    )(place, own, other)


def all_to_all(x, axis, groups=None):
    return lax.all_to_all(x, axis, split_axis=0, concat_axis=0, tiled=True, axis_index_groups=groups)


def shifted(x, by):
    n = lax.axis_size("tm")
    return lax.ppermute(x, "tm", [(i, (i + by) % n) for i in range(n)])


def paired(x, by):
    return lax.ppermute(x, "tm", [(i, i ^ by) for i in range(lax.axis_size("tm"))])


def across(x):
    return lax.ppermute(x, "grid", [(g, g ^ 1) for g in range(Y * Z * C)])


def entering(end, gain, start, i):
    message = jnp.concatenate([end, jnp.broadcast_to(gain, end.shape)])
    total, so_far = jnp.zeros_like(end), jnp.ones_like(end)
    for d in range(1, lax.axis_size("tm")):
        got = shifted(message, d)
        total = total + jnp.where(i >= d, so_far * got[:2], 0.0)
        so_far = so_far * jnp.where(i >= d, got[2:4], 1.0)
    return total + so_far * start


def summed_over_hours(pieces):
    keep0, send0, keep1, send1 = pieces
    q = send0.shape[0] // 2
    wide = lambda v: v.astype(F32)
    got0 = paired(send0, 1)
    got1 = paired(send1, 3)
    last0 = paired((wide(keep0[q:]) + wide(got0[q:])).astype(BF16), 3)
    last1 = paired((wide(keep1[q:]) + wide(got1[:q])).astype(BF16), 1)
    left = wide(keep0[:q]) + wide(got0[:q]) + wide(last0)
    right = wide(keep1[:q]) + wide(got1[q:]) + wide(last1)
    return jnp.concatenate([left, right], axis=1)


def per_device(x0, x1, fading, starting, operator0, operator1):
    grid = lax.axis_size("grid")
    rows, _ = x0.shape
    hours = rows * grid
    scale = (hours * lax.axis_size("tm")) ** -0.5
    core, shard = lax.axis_index("grid") & (C - 1), lax.axis_index("tm")
    place = jnp.stack([core, shard]).astype(jnp.int32)
    n = grid // C
    groups = [[k * C + c for k in range(n)] for c in range(C)]
    packed, *tables = prepare(x0, x1, fading, grid)
    rest = (tables, operator0, operator1, place, core, shard, starting)
    packed, rest = lax.optimization_barrier((packed, rest))
    x = all_to_all(packed, "grid")
    x, (tables, *operators, place, core, shard, starting) = lax.optimization_barrier((x, rest))
    block, since, to_end, gain = tables
    own, other, end, begin = forward(place, x, operators, block, starting)
    enter = entering(end, gain[:, :1], begin, shard)
    enter = enter + across(enter)
    since = lax.dynamic_index_in_dim(since.reshape(2, C, n, rows), core, 1, keepdims=False).transpose(1, 0, 2)
    p = own + across(other) - since[..., None] * enter[None, :, None]
    p, x = lax.optimization_barrier((p.astype(BF16), x))
    p = all_to_all(p, "grid", groups)
    q = p.astype(F32).sum(axis=0).astype(BF16)
    q_own = all_to_all(jnp.broadcast_to(q, p.shape), "grid", groups)
    q_other = across(q_own)
    weight = to_end.reshape(2, grid, rows).transpose(1, 0, 2)[..., None]
    mean = entering((x.astype(F32) * weight).sum(axis=(0, 2)), gain[:, :1], starting, shard)
    w1 = backward(1, place, q_own, q_other, block, x, mean)
    wetness = summed_over_hours(w1) * scale
    sent = lax.dynamic_index_in_dim(cross(place, q_own, q_other).reshape(C, -1, q.shape[2]), core, 0, keepdims=False)
    sent = sent.astype(BF16)
    half = sent.astype(F32)
    for d in range(1, lax.axis_size("tm")):
        half = half + shifted(sent, d).astype(F32)
    partner = across(half)
    middle = jnp.concatenate([jnp.where(core == 0, half, partner), jnp.where(core == 0, partner, half)])
    w0 = backward(0, place, q_own, q_other, block, x, mean)
    warmth = summed_over_hours(w0) * scale
    return warmth, wetness, middle * scale


def solution(mesh):
    return jax.shard_map(
        per_device,
        mesh=mesh,
        in_specs=(
            P(("tm", "grid"), None),
            P(("tm", "grid"), None),
            P(None, "tm"),
            P(None, "grid"),
            P("grid", None),
            P("grid", None),
        ),
        out_specs=(P("tm", "grid"), P("tm", "grid"), P()),
        check_vma=False,
    )
```

```python
import jax
import jax.numpy as jnp
from jax import lax
from jax.experimental import pallas as pl
from jax.experimental.pallas import tpu as pltpu
from jax.sharding import PartitionSpec as P


BLK = 256
NCHUNK = 768
TILE = 256
Y, Z, C = 4, 4, 2
F32, BF16 = jnp.float32, jnp.bfloat16
HIGHEST = lax.Precision.HIGHEST
MIB = 1 << 20


def thirds(v):
    high = v.astype(BF16)
    v = v - high.astype(F32)
    middle = v.astype(BF16)
    return high, middle, (v - middle.astype(F32)).astype(BF16)


def prepare_kernel(x0_ref, x1_ref, fading_ref, out_ref, block_ref, since_ref, to_end_ref, gain_ref, sems):
    n, _, _, width = out_ref.shape

    def copies():
        for i in range(n):
            for f, x_ref in enumerate((x0_ref, x1_ref)):
                yield pltpu.make_async_copy(x_ref.at[:, pl.ds(i * width, width)], out_ref.at[i, f], sems.at[2 * i + f])

    for copy in copies():
        copy.start()
    nb = fading_ref.shape[1] // BLK
    a = jnp.concatenate([fading_ref[f : f + 1, b * BLK : (b + 1) * BLK] for f in range(2) for b in range(nb)])
    log_a = jnp.log(a)
    r = lax.broadcasted_iota(jnp.int32, (BLK, BLK), 0)
    c = lax.broadcasted_iota(jnp.int32, (BLK, BLK), 1)
    upto = jnp.where(r <= c, 1.0, 0.0)
    inclusive = jnp.dot(log_a, upto, precision=HIGHEST, preferred_element_type=F32)
    exclusive = jnp.where(lax.broadcasted_iota(jnp.int32, a.shape, 1) == 0, 0.0, pltpu.roll(inclusive, 1, 1))
    column = exclusive.T
    fresh = 1.0 - a
    total = inclusive[:, BLK - 1 : BLK]
    for f in range(2):
        sums = [total[f * nb + b : f * nb + b + 1] for b in range(nb)]
        ahead = jnp.zeros_like(sums[0])
        for b in range(nb):
            k = f * nb + b
            row = slice(k, k + 1)
            weight = jnp.exp(jnp.minimum(column[:, k : k + 1] - inclusive[row], 0.0)) * fresh[row]
            block_ref[k, :BLK, :BLK] = jnp.where(r == c, 1.0, jnp.where(c < r, -weight, 0.0))
            block_ref[k, :BLK, BLK:] = jnp.broadcast_to(jnp.exp(column[:, k : k + 1]), (BLK, 128))
            last = jnp.exp(sums[b] - inclusive[row]) * fresh[row]
            block_ref[k, BLK:, :BLK] = jnp.broadcast_to(last, (8, BLK))
            block_ref[k, BLK:, BLK:] = jnp.broadcast_to(-jnp.exp(sums[b]), (8, 128))
            behind = sum(sums[b + 1 :], jnp.zeros_like(ahead))
            since_ref[row] = jnp.exp(ahead + exclusive[row])
            to_end_ref[row] = jnp.exp(behind + (sums[b] - inclusive[row])) * fresh[row]
            ahead = ahead + sums[b]
        gain_ref[f : f + 1] = jnp.broadcast_to(jnp.exp(ahead), (1, BLK))
    for copy in copies():
        copy.wait()


def prepare(x0, x1, fading, n):
    rows, points = x0.shape
    width = points // n
    count = fading.size // BLK
    whole = pl.BlockSpec(memory_space=pltpu.VMEM)
    return pl.pallas_call(
        prepare_kernel,
        in_specs=[pl.BlockSpec(memory_space=pl.ANY), pl.BlockSpec(memory_space=pl.ANY), whole],
        out_specs=[pl.BlockSpec(memory_space=pl.ANY), whole, whole, whole, whole],
        out_shape=[
            jax.ShapeDtypeStruct((n, 2, rows, width), x0.dtype),
            jax.ShapeDtypeStruct((count, BLK + 8, BLK + 128), F32),
            jax.ShapeDtypeStruct((count, BLK), F32),
            jax.ShapeDtypeStruct((count, BLK), F32),
            jax.ShapeDtypeStruct((2, BLK), F32),
        ],
        scratch_shapes=[pltpu.SemaphoreType.DMA((2 * n,))],
        compiler_params=pltpu.CompilerParams(vmem_limit_bytes=20 * MIB),
        cost_estimate=pl.CostEstimate(flops=0, bytes_accessed=8 * x0.size, transcendentals=0),
        name="prepare",
    )(x0, x1, fading)


def exact_dot(left, right):
    lh, lm, ll = thirds(left)
    rh, rm, rl = thirds(right)
    return jnp.dot(
        jnp.concatenate([ll, lm, lh, lm, lh, lh], axis=1),
        jnp.concatenate([rh, rm, rl, rh, rm, rh], axis=0),
        preferred_element_type=F32,
    )


def forward_kernel(
    place_ref, x_ref, op0_ref, op1_ref, block_ref, start_ref, p_ref, end_ref, begin_ref, y_ref
):
    f, step = pl.program_id(0), pl.program_id(1)
    count, _, rows, width = x_ref.shape
    hours, rank = y_ref.shape
    nb = hours // BLK
    at = pl.multiple_of(step * (count * rows), count * rows)

    def products(k, op_ref):
        y_ref[pl.ds(at, count * rows)] = jnp.dot(
            x_ref[:, 0].reshape(count * rows, width), op_ref[...], preferred_element_type=F32
        )

        @pl.when(step == 0)
        def _():
            parts = thirds(start_ref[k : k + 1])
            start = jnp.concatenate([part.astype(F32) for part in parts] + [jnp.zeros((5, width), F32)])
            begin = jnp.dot(start.astype(BF16), op_ref[...], preferred_element_type=F32)
            begin_ref[k : k + 1] = begin[0:1] + begin[1:2] + begin[2:3]

    for k, op_ref in enumerate((op0_ref, op1_ref)):

        @pl.when(f == k)
        def _():
            products(k, op_ref)

    @pl.when(step == pl.num_programs(1) - 1)
    def _():
        state = jnp.zeros((1, rank), F32)
        per = BLK // rows
        outs = [exact_dot(block_ref[b, :, :BLK], y_ref[b * BLK : (b + 1) * BLK]) for b in range(nb)]
        for b, out in enumerate(outs):
            out = out - block_ref[b, :, BLK : BLK + 1] * state
            half, at = divmod(b, nb // 2)
            slot = jnp.bitwise_xor(half, place_ref[0])
            p_ref[slot, at * per : (at + 1) * per, 0] = out[:BLK].reshape(per, rows, rank)
            state = out[BLK : BLK + 1]
        end_ref[pl.ds(f, 1)] = state


def forward(place, x, operators, block, starting):
    n, _, rows, width = x.shape
    rank = operators[0].shape[1]
    hours, steps = n * rows, 2
    nb = hours // BLK
    halves = jax.ShapeDtypeStruct((2, n // 2, 2, rows, rank), F32)
    halves_spec = pl.BlockSpec((2, n // 2, 1, rows, rank), lambda f, i: (0, 0, f, 0, 0))
    pair, pair_spec = jax.ShapeDtypeStruct((2, rank), F32), pl.BlockSpec((2, rank), lambda f, i: (0, 0))
    op_spec = pl.BlockSpec((width, rank), lambda f, i: (0, 0))
    return pl.pallas_call(
        forward_kernel,
        grid=(2, steps),
        in_specs=[
            pl.BlockSpec(memory_space=pltpu.SMEM),
            pl.BlockSpec((n // steps, 1, rows, width), lambda f, i: (i, f, 0, 0)),
            op_spec,
            op_spec,
            pl.BlockSpec((nb, BLK + 8, BLK + 128), lambda f, i: (f, 0, 0)),
            pl.BlockSpec((2, width), lambda f, i: (0, 0)),
        ],
        out_specs=[halves_spec, pair_spec, pair_spec],
        out_shape=[halves, pair, pair],
        scratch_shapes=[pltpu.VMEM((hours, rank), F32)],
        compiler_params=pltpu.CompilerParams(vmem_limit_bytes=24 * MIB),
        cost_estimate=pl.CostEstimate(
            flops=4 * hours * width * rank, bytes_accessed=4 * hours * width, transcendentals=0
        ),
        name="forward",
    )(place, x, *operators, block, starting)


def backward_kernel(
    place_ref, own_ref, other_ref, block_ref, x_ref, enter_ref, keep0_ref, send0_ref, keep1_ref, send1_ref, z_ref, carried, w_ref
):
    step = pl.program_id(0)
    rank = own_ref.shape[3]
    quarter = rank // 4

    @pl.when(step == 0)
    def _():
        nb = block_ref.shape[0]
        rows = own_ref.shape[2]
        per = BLK // rows
        reverse = jnp.zeros((rank, 1), F32)

        def placed(ref, value, cols, base=0):
            for order in range(2):
                for d in range(4):
                    to = jnp.bitwise_xor(d, place_ref[1])
                    if order == 0:
                        to = jnp.where(to == 0, 0, to % 3 + 1)
                    at = pl.multiple_of(base + to * quarter, quarter)
                    ref[order, pl.ds(at, quarter), cols] = value[d * quarter : (d + 1) * quarter]

        parts = []
        for b in range(nb):
            half, at = divmod(b, nb // 2)
            own = own_ref[at * per : (at + 1) * per, 0].reshape(BLK, rank)
            other = other_ref[at * per : (at + 1) * per, 0].reshape(BLK, rank)
            q = jnp.where(place_ref[0] == half, own.astype(F32), other.astype(F32)).T.astype(BF16)
            high, middle, low = thirds(block_ref[b, :BLK])
            parts.append(
                jnp.dot(
                    jnp.concatenate([q, q, q], axis=1),
                    jnp.concatenate([low, middle, high], axis=0),
                    preferred_element_type=F32,
                )
            )
        for b in reversed(range(nb)):
            out = parts[b] - reverse * block_ref[b, BLK : BLK + 1, :]
            z = out[:, :BLK]
            high = z.astype(BF16)
            cols = slice(b * BLK, (b + 1) * BLK)
            placed(z_ref, high, cols)
            placed(z_ref, (z - high.astype(F32)).astype(BF16), cols, rank)
            reverse = out[:, BLK : BLK + 1]
        placed(carried, jnp.broadcast_to(reverse, carried.shape[1:]), slice(0, carried.shape[2]))

    hours = z_ref.shape[2]
    order = step // (pl.num_programs(0) // 2)
    for t in range(x_ref.shape[3] // TILE):
        cols = slice(t * TILE, (t + 1) * TILE)
        w = jnp.dot(z_ref[order], x_ref[:, 0, :, cols].reshape(hours, TILE), preferred_element_type=F32)
        w = w[:rank] + w[rank:] - carried[order][:, 0:1] * enter_ref[0, :, cols]
        w_ref[:, cols] = w.astype(BF16)
    for k, (keep_ref, send_ref) in enumerate(((keep0_ref, send0_ref), (keep1_ref, send1_ref))):

        @pl.when(order == k)
        def _():
            keep_ref[...] = w_ref[: rank // 2]
            send_ref[...] = w_ref[rank // 2 :]


def backward(f, place, own, other, block, x, enter):
    n, _, rows, width = x.shape
    hours, rank = n * rows, own.shape[3]
    nb = hours // BLK
    steps = width // NCHUNK // 2
    q_spec = pl.BlockSpec((n // 2, 1, rows, rank), lambda i: (0, 1 - f, 0, 0))
    left = pl.BlockSpec((rank // 2, NCHUNK), lambda i: (0, jnp.minimum(i, steps - 1)))
    right = pl.BlockSpec((rank // 2, NCHUNK), lambda i: (0, jnp.maximum(i - steps, 0)))
    piece = jax.ShapeDtypeStruct((rank // 2, width // 2), BF16)
    return pl.pallas_call(
        backward_kernel,
        grid=(2 * steps,),
        in_specs=[
            pl.BlockSpec(memory_space=pltpu.SMEM),
            q_spec,
            q_spec,
            pl.BlockSpec((nb, BLK + 8, BLK + 128), lambda i: (f, 0, 0)),
            pl.BlockSpec((n, 1, rows, NCHUNK), lambda i: (0, f, 0, i)),
            pl.BlockSpec((1, 1, NCHUNK), lambda i: (f, 0, i)),
        ],
        out_specs=[left, left, right, right],
        out_shape=[piece] * 4,
        scratch_shapes=[
            pltpu.VMEM((2, 2 * rank, hours), BF16),
            pltpu.VMEM((2, rank, 128), F32),
            pltpu.VMEM((rank, NCHUNK), BF16),
        ],
        compiler_params=pltpu.CompilerParams(vmem_limit_bytes=54 * MIB),
        cost_estimate=pl.CostEstimate(
            flops=4 * hours * width * rank, bytes_accessed=2 * hours * width, transcendentals=0
        ),
        name="backward",
    )(place, own, other, block, x, enter[:, None])


def cross_kernel(place_ref, own_ref, other_ref, out_ref):
    n, _, rows, rank = own_ref.shape
    out = jnp.zeros(out_ref.shape, F32)
    for ref in (own_ref, other_ref):
        left = ref[:, 0].reshape(n * rows, rank).astype(F32).T.astype(BF16)
        out = out + jnp.dot(left, ref[:, 1].reshape(n * rows, rank), preferred_element_type=F32)
    out_ref[...] = out


def cross(place, own, other):
    rank = own.shape[3]
    whole = pl.BlockSpec(memory_space=pltpu.VMEM)
    return pl.pallas_call(
        cross_kernel,
        out_shape=jax.ShapeDtypeStruct((rank, rank), F32),
        in_specs=[pl.BlockSpec(memory_space=pltpu.SMEM), whole, whole],
        out_specs=whole,
        compiler_params=pltpu.CompilerParams(vmem_limit_bytes=8 * MIB),
        cost_estimate=pl.CostEstimate(flops=2 * own.size * rank, bytes_accessed=4 * own.size, transcendentals=0),
        name="cross",
    )(place, own, other)


def all_to_all(x, axis, groups=None):
    return lax.all_to_all(x, axis, split_axis=0, concat_axis=0, tiled=True, axis_index_groups=groups)


def shifted(x, by):
    n = lax.axis_size("tm")
    return lax.ppermute(x, "tm", [(i, (i + by) % n) for i in range(n)])


def paired(x, by):
    return lax.ppermute(x, "tm", [(i, i ^ by) for i in range(lax.axis_size("tm"))])


def across(x):
    return lax.ppermute(x, "grid", [(g, g ^ 1) for g in range(Y * Z * C)])


def entering(end, gain, start, i):
    message = jnp.concatenate([end, jnp.broadcast_to(gain, end.shape)])
    total, so_far = jnp.zeros_like(end), jnp.ones_like(end)
    for d in range(1, lax.axis_size("tm")):
        got = shifted(message, d)
        total = total + jnp.where(i >= d, so_far * got[:2], 0.0)
        so_far = so_far * jnp.where(i >= d, got[2:4], 1.0)
    return total + so_far * start


def summed_over_hours(pieces):
    keep0, send0, keep1, send1 = pieces
    q = send0.shape[0] // 2
    wide = lambda v: v.astype(F32)
    got0 = paired(send0, 1)
    got1 = paired(send1, 3)
    sent0 = (wide(keep0[q:]) + wide(got0[q:])).astype(BF16)
    sent1 = (wide(keep1[q:]) + wide(got1[:q])).astype(BF16)
    last0, last1 = paired(sent0, 3), paired(sent1, 1)
    left = wide(keep0[:q]) + wide(got0[:q]) + wide(last0)
    right = wide(keep1[:q]) + wide(got1[q:]) + wide(last1)
    return jnp.concatenate([left, right], axis=1), (sent0, sent1)


def per_device(x0, x1, fading, starting, operator0, operator1):
    grid = lax.axis_size("grid")
    rows, _ = x0.shape
    hours = rows * grid
    scale = (hours * lax.axis_size("tm")) ** -0.5
    core, shard = lax.axis_index("grid") & (C - 1), lax.axis_index("tm")
    place = jnp.stack([core, shard]).astype(jnp.int32)
    n = grid // C
    groups = [[k * C + c for k in range(n)] for c in range(C)]
    packed, *tables = prepare(x0, x1, fading, grid)
    rest = (tables, operator0, operator1, place, core, shard, starting)
    packed, rest = lax.optimization_barrier((packed, rest))
    x = all_to_all(packed, "grid")
    x, (tables, *operators, place, core, shard, starting) = lax.optimization_barrier((x, rest))
    block, since, to_end, gain = tables
    (own, other), end, begin = forward(place, x, operators, block, starting)
    enter = entering(end, gain[:, :1], begin, shard)
    enter = enter + across(enter)
    since = lax.dynamic_index_in_dim(since.reshape(2, C, n, rows), core, 1, keepdims=False).transpose(1, 0, 2)
    p = own + across(other) - since[..., None] * enter[None, :, None]
    p, x = lax.optimization_barrier((p.astype(BF16), x))
    p = all_to_all(p, "grid", groups)
    q = p.astype(F32).sum(axis=0).astype(BF16)
    q_own = all_to_all(jnp.broadcast_to(q, p.shape), "grid", groups)
    q_other = across(q_own)
    weight = to_end.reshape(2, grid, rows).transpose(1, 0, 2)[..., None]
    mean = entering((x.astype(F32) * weight).sum(axis=(0, 2)), gain[:, :1], starting, shard)
    w1 = backward(1, place, q_own, q_other, block, x, mean)
    wetness = summed_over_hours(w1)[0] * scale
    w0 = backward(0, place, q_own, q_other, block, x, mean)
    warmth, last = summed_over_hours(w0)
    warmth = warmth * scale
    sent = cross(place, q_own, q_other).reshape(C, -1, q.shape[2])
    sent = lax.dynamic_index_in_dim(sent, core, 0, keepdims=False).astype(BF16)
    got = [shifted(sent, d) for d in range(1, lax.axis_size("tm"))]
    got, _ = lax.optimization_barrier((got, last))
    half = sum((part.astype(F32) for part in got), sent.astype(F32))
    partner = across(half)
    middle = jnp.concatenate([jnp.where(core == 0, half, partner), jnp.where(core == 0, partner, half)])
    return warmth, wetness, middle * scale


def solution(mesh):
    return jax.shard_map(
        per_device,
        mesh=mesh,
        in_specs=(
            P(("tm", "grid"), None),
            P(("tm", "grid"), None),
            P(None, "tm"),
            P(None, "grid"),
            P("grid", None),
            P("grid", None),
        ),
        out_specs=(P("tm", "grid"), P("tm", "grid"), P()),
        check_vma=False,
    )
```

```python
import functools

import jax
import jax.numpy as jnp
from jax import lax
from jax.experimental import pallas as pl
from jax.experimental.pallas import tpu as pltpu
from jax.sharding import PartitionSpec as P


BLK = 256
NCHUNK = 768
TILE = 256
Y, Z, C = 4, 4, 2
F32, BF16 = jnp.float32, jnp.bfloat16
HIGHEST = lax.Precision.HIGHEST
MIB = 1 << 20


def thirds(v):
    high = v.astype(BF16)
    v = v - high.astype(F32)
    middle = v.astype(BF16)
    return high, middle, (v - middle.astype(F32)).astype(BF16)


def prepare_kernel(x0_ref, x1_ref, fading_ref, out_ref, block_ref, since_ref, to_end_ref, gain_ref, sems):
    n, _, _, width = out_ref.shape

    def copies():
        for i in range(n):
            for f, x_ref in enumerate((x0_ref, x1_ref)):
                yield pltpu.make_async_copy(x_ref.at[:, pl.ds(i * width, width)], out_ref.at[i, f], sems.at[2 * i + f])

    for copy in copies():
        copy.start()
    nb = fading_ref.shape[1] // BLK
    a = jnp.concatenate([fading_ref[f : f + 1, b * BLK : (b + 1) * BLK] for f in range(2) for b in range(nb)])
    log_a = jnp.log(a)
    r = lax.broadcasted_iota(jnp.int32, (BLK, BLK), 0)
    c = lax.broadcasted_iota(jnp.int32, (BLK, BLK), 1)
    upto = jnp.where(r <= c, 1.0, 0.0)
    inclusive = jnp.dot(log_a, upto, precision=HIGHEST, preferred_element_type=F32)
    exclusive = jnp.where(lax.broadcasted_iota(jnp.int32, a.shape, 1) == 0, 0.0, pltpu.roll(inclusive, 1, 1))
    column = exclusive.T
    fresh = 1.0 - a
    total = inclusive[:, BLK - 1 : BLK]
    for f in range(2):
        sums = [total[f * nb + b : f * nb + b + 1] for b in range(nb)]
        ahead = jnp.zeros_like(sums[0])
        for b in range(nb):
            k = f * nb + b
            row = slice(k, k + 1)
            weight = jnp.exp(jnp.minimum(column[:, k : k + 1] - inclusive[row], 0.0)) * fresh[row]
            block_ref[k, :BLK, :BLK] = jnp.where(r == c, 1.0, jnp.where(c < r, -weight, 0.0))
            block_ref[k, :BLK, BLK:] = jnp.broadcast_to(jnp.exp(column[:, k : k + 1]), (BLK, 128))
            last = jnp.exp(sums[b] - inclusive[row]) * fresh[row]
            block_ref[k, BLK:, :BLK] = jnp.broadcast_to(last, (8, BLK))
            block_ref[k, BLK:, BLK:] = jnp.broadcast_to(-jnp.exp(sums[b]), (8, 128))
            behind = sum(sums[b + 1 :], jnp.zeros_like(ahead))
            since_ref[row] = jnp.exp(ahead + exclusive[row])
            to_end_ref[row] = jnp.exp(behind + (sums[b] - inclusive[row])) * fresh[row]
            ahead = ahead + sums[b]
        gain_ref[f : f + 1] = jnp.broadcast_to(jnp.exp(ahead), (1, BLK))
    for copy in copies():
        copy.wait()


def prepare(x0, x1, fading, n):
    rows, points = x0.shape
    width = points // n
    count = fading.size // BLK
    whole = pl.BlockSpec(memory_space=pltpu.VMEM)
    return pl.pallas_call(
        prepare_kernel,
        in_specs=[pl.BlockSpec(memory_space=pl.ANY), pl.BlockSpec(memory_space=pl.ANY), whole],
        out_specs=[pl.BlockSpec(memory_space=pl.ANY), whole, whole, whole, whole],
        out_shape=[
            jax.ShapeDtypeStruct((n, 2, rows, width), x0.dtype),
            jax.ShapeDtypeStruct((count, BLK + 8, BLK + 128), F32),
            jax.ShapeDtypeStruct((count, BLK), F32),
            jax.ShapeDtypeStruct((count, BLK), F32),
            jax.ShapeDtypeStruct((2, BLK), F32),
        ],
        scratch_shapes=[pltpu.SemaphoreType.DMA((2 * n,))],
        compiler_params=pltpu.CompilerParams(vmem_limit_bytes=20 * MIB),
        cost_estimate=pl.CostEstimate(flops=0, bytes_accessed=8 * x0.size, transcendentals=0),
        name="prepare",
    )(x0, x1, fading)


def exact_dot(left, right):
    lh, lm, ll = thirds(left)
    rh, rm, rl = thirds(right)
    return jnp.dot(
        jnp.concatenate([ll, lm, lh, lm, lh, lh], axis=1),
        jnp.concatenate([rh, rm, rl, rh, rm, rh], axis=0),
        preferred_element_type=F32,
    )


def forward_kernel(
    place_ref, x_ref, op0_ref, op1_ref, block_ref, start_ref, p_ref, end_ref, begin_ref, y_ref
):
    f, step = pl.program_id(0), pl.program_id(1)
    count, _, rows, width = x_ref.shape
    hours, rank = y_ref.shape
    nb = hours // BLK
    at = pl.multiple_of(step * (count * rows), count * rows)

    def products(k, op_ref):
        y_ref[pl.ds(at, count * rows)] = jnp.dot(
            x_ref[:, 0].reshape(count * rows, width), op_ref[...], preferred_element_type=F32
        )

        @pl.when(step == 0)
        def _():
            parts = thirds(start_ref[k : k + 1])
            start = jnp.concatenate([part.astype(F32) for part in parts] + [jnp.zeros((5, width), F32)])
            begin = jnp.dot(start.astype(BF16), op_ref[...], preferred_element_type=F32)
            begin_ref[k : k + 1] = begin[0:1] + begin[1:2] + begin[2:3]

    for k, op_ref in enumerate((op0_ref, op1_ref)):

        @pl.when(f == k)
        def _():
            products(k, op_ref)

    @pl.when(step == pl.num_programs(1) - 1)
    def _():
        state = jnp.zeros((1, rank), F32)
        per = BLK // rows
        outs = [exact_dot(block_ref[b, :, :BLK], y_ref[b * BLK : (b + 1) * BLK]) for b in range(nb)]
        for b, out in enumerate(outs):
            out = out - block_ref[b, :, BLK : BLK + 1] * state
            half, at = divmod(b, nb // 2)
            slot = jnp.bitwise_xor(half, place_ref[0])
            p_ref[slot, at * per : (at + 1) * per, 0] = out[:BLK].reshape(per, rows, rank)
            state = out[BLK : BLK + 1]
        end_ref[pl.ds(f, 1)] = state


def forward(place, x, operators, block, starting):
    n, _, rows, width = x.shape
    rank = operators[0].shape[1]
    hours, steps = n * rows, 2
    nb = hours // BLK
    halves = jax.ShapeDtypeStruct((2, n // 2, 2, rows, rank), F32)
    halves_spec = pl.BlockSpec((2, n // 2, 1, rows, rank), lambda f, i: (0, 0, f, 0, 0))
    pair, pair_spec = jax.ShapeDtypeStruct((2, rank), F32), pl.BlockSpec((2, rank), lambda f, i: (0, 0))
    op_spec = pl.BlockSpec((width, rank), lambda f, i: (0, 0))
    return pl.pallas_call(
        forward_kernel,
        grid=(2, steps),
        in_specs=[
            pl.BlockSpec(memory_space=pltpu.SMEM),
            pl.BlockSpec((n // steps, 1, rows, width), lambda f, i: (i, f, 0, 0)),
            op_spec,
            op_spec,
            pl.BlockSpec((nb, BLK + 8, BLK + 128), lambda f, i: (f, 0, 0)),
            pl.BlockSpec((2, width), lambda f, i: (0, 0)),
        ],
        out_specs=[halves_spec, pair_spec, pair_spec],
        out_shape=[halves, pair, pair],
        scratch_shapes=[pltpu.VMEM((hours, rank), F32)],
        compiler_params=pltpu.CompilerParams(vmem_limit_bytes=24 * MIB),
        cost_estimate=pl.CostEstimate(
            flops=4 * hours * width * rank, bytes_accessed=4 * hours * width, transcendentals=0
        ),
        name="forward",
    )(place, x, *operators, block, starting)


def backward_kernel(
    f, place_ref, own_ref, other_ref, block_ref, x_ref, enter_ref, keep0_ref, send0_ref, keep1_ref, send1_ref, z_ref, carried, w_ref,
    held, sems,
):
    step = pl.program_id(0)
    rank = own_ref.shape[3]
    quarter = rank // 4

    count, _, _, chunk = held.shape

    def load(i):
        return pltpu.make_async_copy(x_ref.at[:, f, :, pl.ds(i * chunk, chunk)], held.at[i], sems.at[i])

    @pl.when(step == 0)
    def _():
        for i in range(count):
            load(i).start()
        nb = block_ref.shape[0]
        rows = own_ref.shape[2]
        per = BLK // rows
        reverse = jnp.zeros((rank, 1), F32)

        def placed(ref, value, cols, base=0):
            for order in range(2):
                for d in range(4):
                    to = jnp.bitwise_xor(d, place_ref[1])
                    if order == 0:
                        to = jnp.where(to == 0, 0, to % 3 + 1)
                    at = pl.multiple_of(base + to * quarter, quarter)
                    ref[order, pl.ds(at, quarter), cols] = value[d * quarter : (d + 1) * quarter]

        parts = []
        for b in range(nb):
            half, at = divmod(b, nb // 2)
            own = own_ref[at * per : (at + 1) * per, 0].reshape(BLK, rank)
            other = other_ref[at * per : (at + 1) * per, 0].reshape(BLK, rank)
            q = jnp.where(place_ref[0] == half, own.astype(F32), other.astype(F32)).T.astype(BF16)
            high, middle, low = thirds(block_ref[b, :BLK])
            parts.append(
                jnp.dot(
                    jnp.concatenate([q, q, q], axis=1),
                    jnp.concatenate([low, middle, high], axis=0),
                    preferred_element_type=F32,
                )
            )
        for b in reversed(range(nb)):
            out = parts[b] - reverse * block_ref[b, BLK : BLK + 1, :]
            z = out[:, :BLK]
            high = z.astype(BF16)
            cols = slice(b * BLK, (b + 1) * BLK)
            placed(z_ref, high, cols)
            placed(z_ref, (z - high.astype(F32)).astype(BF16), cols, rank)
            reverse = out[:, BLK : BLK + 1]
        placed(carried, jnp.broadcast_to(reverse, carried.shape[1:]), slice(0, carried.shape[2]))

    load(step).wait()
    hours = z_ref.shape[2]
    order = step // (pl.num_programs(0) // 2)
    for t in range(chunk // TILE):
        cols = slice(t * TILE, (t + 1) * TILE)
        w = jnp.dot(z_ref[order], held[step, :, :, cols].reshape(hours, TILE), preferred_element_type=F32)
        w = w[:rank] + w[rank:] - carried[order][:, 0:1] * enter_ref[0, :, cols]
        w_ref[:, cols] = w.astype(BF16)
    for k, (keep_ref, send_ref) in enumerate(((keep0_ref, send0_ref), (keep1_ref, send1_ref))):

        @pl.when(order == k)
        def _():
            keep_ref[...] = w_ref[: rank // 2]
            send_ref[...] = w_ref[rank // 2 :]


def backward(f, place, own, other, block, x, enter):
    n, _, rows, width = x.shape
    hours, rank = n * rows, own.shape[3]
    nb = hours // BLK
    steps = width // NCHUNK // 2
    q_spec = pl.BlockSpec((n // 2, 1, rows, rank), lambda i: (0, 1 - f, 0, 0))
    left = pl.BlockSpec((rank // 2, NCHUNK), lambda i: (0, jnp.minimum(i, steps - 1)))
    right = pl.BlockSpec((rank // 2, NCHUNK), lambda i: (0, jnp.maximum(i - steps, 0)))
    piece = jax.ShapeDtypeStruct((rank // 2, width // 2), BF16)
    return pl.pallas_call(
        functools.partial(backward_kernel, f),
        grid=(2 * steps,),
        in_specs=[
            pl.BlockSpec(memory_space=pltpu.SMEM),
            q_spec,
            q_spec,
            pl.BlockSpec((nb, BLK + 8, BLK + 128), lambda i: (f, 0, 0)),
            pl.BlockSpec(memory_space=pl.ANY),
            pl.BlockSpec((1, 1, NCHUNK), lambda i: (f, 0, i)),
        ],
        out_specs=[left, left, right, right],
        out_shape=[piece] * 4,
        scratch_shapes=[
            pltpu.VMEM((2, 2 * rank, hours), BF16),
            pltpu.VMEM((2, rank, 128), F32),
            pltpu.VMEM((rank, NCHUNK), BF16),
            pltpu.VMEM((2 * steps, n, rows, NCHUNK), BF16),
            pltpu.SemaphoreType.DMA((2 * steps,)),
        ],
        compiler_params=pltpu.CompilerParams(vmem_limit_bytes=51 * MIB),
        cost_estimate=pl.CostEstimate(
            flops=4 * hours * width * rank, bytes_accessed=2 * hours * width, transcendentals=0
        ),
        name="backward",
    )(place, own, other, block, x, enter[:, None])


def cross_kernel(place_ref, own_ref, other_ref, out_ref):
    n, _, rows, rank = own_ref.shape
    out = jnp.zeros(out_ref.shape, F32)
    for ref in (own_ref, other_ref):
        left = ref[:, 0].reshape(n * rows, rank).astype(F32).T.astype(BF16)
        out = out + jnp.dot(left, ref[:, 1].reshape(n * rows, rank), preferred_element_type=F32)
    out_ref[...] = out


def cross(place, own, other):
    rank = own.shape[3]
    whole = pl.BlockSpec(memory_space=pltpu.VMEM)
    return pl.pallas_call(
        cross_kernel,
        out_shape=jax.ShapeDtypeStruct((rank, rank), F32),
        in_specs=[pl.BlockSpec(memory_space=pltpu.SMEM), whole, whole],
        out_specs=whole,
        compiler_params=pltpu.CompilerParams(vmem_limit_bytes=8 * MIB),
        cost_estimate=pl.CostEstimate(flops=2 * own.size * rank, bytes_accessed=4 * own.size, transcendentals=0),
        name="cross",
    )(place, own, other)


def all_to_all(x, axis, groups=None):
    return lax.all_to_all(x, axis, split_axis=0, concat_axis=0, tiled=True, axis_index_groups=groups)


def shifted(x, by):
    n = lax.axis_size("tm")
    return lax.ppermute(x, "tm", [(i, (i + by) % n) for i in range(n)])


def paired(x, by):
    return lax.ppermute(x, "tm", [(i, i ^ by) for i in range(lax.axis_size("tm"))])


def across(x):
    return lax.ppermute(x, "grid", [(g, g ^ 1) for g in range(Y * Z * C)])


def entering(end, gain, start, i):
    message = jnp.concatenate([end, jnp.broadcast_to(gain, end.shape)])
    total, so_far = jnp.zeros_like(end), jnp.ones_like(end)
    for d in range(1, lax.axis_size("tm")):
        got = shifted(message, d)
        total = total + jnp.where(i >= d, so_far * got[:2], 0.0)
        so_far = so_far * jnp.where(i >= d, got[2:4], 1.0)
    return total + so_far * start


def summed_over_hours(pieces):
    keep0, send0, keep1, send1 = pieces
    q = send0.shape[0] // 2
    wide = lambda v: v.astype(F32)
    got0 = paired(send0, 1)
    got1 = paired(send1, 3)
    sent0 = (wide(keep0[q:]) + wide(got0[q:])).astype(BF16)
    sent1 = (wide(keep1[q:]) + wide(got1[:q])).astype(BF16)
    last0, last1 = paired(sent0, 3), paired(sent1, 1)
    left = wide(keep0[:q]) + wide(got0[:q]) + wide(last0)
    right = wide(keep1[:q]) + wide(got1[q:]) + wide(last1)
    return jnp.concatenate([left, right], axis=1), (sent0, sent1)


def per_device(x0, x1, fading, starting, operator0, operator1):
    grid = lax.axis_size("grid")
    rows, _ = x0.shape
    hours = rows * grid
    scale = (hours * lax.axis_size("tm")) ** -0.5
    core, shard = lax.axis_index("grid") & (C - 1), lax.axis_index("tm")
    place = jnp.stack([core, shard]).astype(jnp.int32)
    n = grid // C
    groups = [[k * C + c for k in range(n)] for c in range(C)]
    packed, *tables = prepare(x0, x1, fading, grid)
    rest = (tables, operator0, operator1, place, core, shard, starting)
    packed, rest = lax.optimization_barrier((packed, rest))
    x = all_to_all(packed, "grid")
    x, (tables, *operators, place, core, shard, starting) = lax.optimization_barrier((x, rest))
    block, since, to_end, gain = tables
    (own, other), end, begin = forward(place, x, operators, block, starting)
    enter = entering(end, gain[:, :1], begin, shard)
    enter = enter + across(enter)
    since = lax.dynamic_index_in_dim(since.reshape(2, C, n, rows), core, 1, keepdims=False).transpose(1, 0, 2)
    p = own + across(other) - since[..., None] * enter[None, :, None]
    p, x = lax.optimization_barrier((p.astype(BF16), x))
    p = all_to_all(p, "grid", groups)
    q = p.astype(F32).sum(axis=0).astype(BF16)
    q_own = all_to_all(jnp.broadcast_to(q, p.shape), "grid", groups)
    q_other = across(q_own)
    weight = to_end.reshape(2, grid, rows).transpose(1, 0, 2)[..., None]
    mean = entering((x.astype(F32) * weight).sum(axis=(0, 2)), gain[:, :1], starting, shard)
    w1 = backward(1, place, q_own, q_other, block, x, mean)
    wetness = summed_over_hours(w1)[0] * scale
    w0 = backward(0, place, q_own, q_other, block, x, mean)
    warmth, last = summed_over_hours(w0)
    warmth = warmth * scale
    sent = cross(place, q_own, q_other).reshape(C, -1, q.shape[2])
    sent = lax.dynamic_index_in_dim(sent, core, 0, keepdims=False).astype(BF16)
    got = [shifted(sent, d) for d in range(1, lax.axis_size("tm"))]
    got, _ = lax.optimization_barrier((got, last))
    half = sum((part.astype(F32) for part in got), sent.astype(F32))
    partner = across(half)
    middle = jnp.concatenate([jnp.where(core == 0, half, partner), jnp.where(core == 0, partner, half)])
    return warmth, wetness, middle * scale


def solution(mesh):
    return jax.shard_map(
        per_device,
        mesh=mesh,
        in_specs=(
            P(("tm", "grid"), None),
            P(("tm", "grid"), None),
            P(None, "tm"),
            P(None, "grid"),
            P("grid", None),
            P("grid", None),
        ),
        out_specs=(P("tm", "grid"), P("tm", "grid"), P()),
        check_vma=False,
    )
```

```python
import functools

import jax
import jax.numpy as jnp
from jax import lax
from jax.experimental import pallas as pl
from jax.experimental.pallas import tpu as pltpu
from jax.sharding import PartitionSpec as P


BLK = 256
HALF = BLK // 2
NCHUNK = 768
TILE = 256
Y, Z, C = 4, 4, 2
F32, BF16 = jnp.float32, jnp.bfloat16
HIGHEST = lax.Precision.HIGHEST
MIB = 1 << 20


def thirds(v):
    high = v.astype(BF16)
    v = v - high.astype(F32)
    middle = v.astype(BF16)
    return high, middle, (v - middle.astype(F32)).astype(BF16)


def prepare_kernel(x0_ref, x1_ref, fading_ref, out_ref, block_ref, since_ref, to_end_ref, gain_ref, sems):
    n, _, _, width = out_ref.shape

    def copies():
        for i in range(n):
            for f, x_ref in enumerate((x0_ref, x1_ref)):
                yield pltpu.make_async_copy(x_ref.at[:, pl.ds(i * width, width)], out_ref.at[i, f], sems.at[2 * i + f])

    for copy in copies():
        copy.start()
    nb = fading_ref.shape[1] // BLK
    a = jnp.concatenate([fading_ref[f : f + 1, b * BLK : (b + 1) * BLK] for f in range(2) for b in range(nb)])
    log_a = jnp.log(a)
    r = lax.broadcasted_iota(jnp.int32, (BLK, BLK), 0)
    c = lax.broadcasted_iota(jnp.int32, (BLK, BLK), 1)
    upto = jnp.where(r <= c, 1.0, 0.0)
    r, c = r[:HALF, :HALF], c[:HALF, :HALF]
    inclusive = jnp.dot(log_a, upto, precision=HIGHEST, preferred_element_type=F32)
    exclusive = jnp.where(lax.broadcasted_iota(jnp.int32, a.shape, 1) == 0, 0.0, pltpu.roll(inclusive, 1, 1))
    column = exclusive.T
    fresh = 1.0 - a
    total = inclusive[:, BLK - 1 : BLK]
    for f in range(2):
        sums = [total[f * nb + b : f * nb + b + 1] for b in range(nb)]
        ahead = jnp.zeros_like(sums[0])
        for b in range(nb):
            k = f * nb + b
            row = slice(k, k + 1)
            for i in range(2):
                for j in range(2):
                    down, over = slice(i * HALF, (i + 1) * HALF), slice(j * HALF, (j + 1) * HALF)
                    if i < j:
                        block_ref[k, down, over] = jnp.zeros((HALF, HALF), F32)
                        continue
                    spread = column[down, k : k + 1] - inclusive[row, over]
                    weight = jnp.exp(jnp.minimum(spread, 0.0)) * -fresh[row, over]
                    block_ref[k, down, over] = jnp.where(r == c, 1.0, jnp.where(c < r, weight, 0.0)) if i == j else weight
            block_ref[k, :BLK, BLK:] = jnp.broadcast_to(jnp.exp(column[:, k : k + 1]), (BLK, 128))
            last = jnp.exp(sums[b] - inclusive[row]) * fresh[row]
            block_ref[k, BLK:, :BLK] = jnp.broadcast_to(last, (8, BLK))
            block_ref[k, BLK:, BLK:] = jnp.broadcast_to(-jnp.exp(sums[b]), (8, 128))
            behind = sum(sums[b + 1 :], jnp.zeros_like(ahead))
            since_ref[row] = jnp.exp(ahead + exclusive[row])
            to_end_ref[row] = jnp.exp(behind + (sums[b] - inclusive[row])) * fresh[row]
            ahead = ahead + sums[b]
        gain_ref[f : f + 1] = jnp.broadcast_to(jnp.exp(ahead), (1, BLK))
    for copy in copies():
        copy.wait()


def prepare(x0, x1, fading, n):
    rows, points = x0.shape
    width = points // n
    count = fading.size // BLK
    whole = pl.BlockSpec(memory_space=pltpu.VMEM)
    return pl.pallas_call(
        prepare_kernel,
        in_specs=[pl.BlockSpec(memory_space=pl.ANY), pl.BlockSpec(memory_space=pl.ANY), whole],
        out_specs=[pl.BlockSpec(memory_space=pl.ANY), whole, whole, whole, whole],
        out_shape=[
            jax.ShapeDtypeStruct((n, 2, rows, width), x0.dtype),
            jax.ShapeDtypeStruct((count, BLK + 8, BLK + 128), F32),
            jax.ShapeDtypeStruct((count, BLK), F32),
            jax.ShapeDtypeStruct((count, BLK), F32),
            jax.ShapeDtypeStruct((2, BLK), F32),
        ],
        scratch_shapes=[pltpu.SemaphoreType.DMA((2 * n,))],
        compiler_params=pltpu.CompilerParams(vmem_limit_bytes=20 * MIB),
        cost_estimate=pl.CostEstimate(flops=0, bytes_accessed=8 * x0.size, transcendentals=0),
        name="prepare",
    )(x0, x1, fading)


def exact_dot(left, right):
    lh, lm, ll = thirds(left)
    rh, rm, rl = thirds(right)
    return jnp.dot(
        jnp.concatenate([ll, lm, lh, lm, lh, lh], axis=1),
        jnp.concatenate([rh, rm, rl, rh, rm, rh], axis=0),
        preferred_element_type=F32,
    )


def forward_kernel(
    place_ref, x_ref, op0_ref, op1_ref, block_ref, start_ref, p_ref, end_ref, begin_ref, y_ref
):
    f, step = pl.program_id(0), pl.program_id(1)
    count, _, rows, width = x_ref.shape
    hours, rank = y_ref.shape
    nb = hours // BLK
    at = pl.multiple_of(step * (count * rows), count * rows)

    def products(k, op_ref):
        y_ref[pl.ds(at, count * rows)] = jnp.dot(
            x_ref[:, 0].reshape(count * rows, width), op_ref[...], preferred_element_type=F32
        )

        @pl.when(step == 0)
        def _():
            parts = thirds(start_ref[k : k + 1])
            start = jnp.concatenate([part.astype(F32) for part in parts] + [jnp.zeros((5, width), F32)])
            begin = jnp.dot(start.astype(BF16), op_ref[...], preferred_element_type=F32)
            begin_ref[k : k + 1] = begin[0:1] + begin[1:2] + begin[2:3]

    for k, op_ref in enumerate((op0_ref, op1_ref)):

        @pl.when(f == k)
        def _():
            products(k, op_ref)

    @pl.when(step == pl.num_programs(1) - 1)
    def _():
        state = jnp.zeros((1, rank), F32)
        per = BLK // rows
        outs = [exact_dot(block_ref[b, :, :BLK], y_ref[b * BLK : (b + 1) * BLK]) for b in range(nb)]
        for b, out in enumerate(outs):
            out = out - block_ref[b, :, BLK : BLK + 1] * state
            half, at = divmod(b, nb // 2)
            slot = jnp.bitwise_xor(half, place_ref[0])
            p_ref[slot, at * per : (at + 1) * per, 0] = out[:BLK].reshape(per, rows, rank)
            state = out[BLK : BLK + 1]
        end_ref[pl.ds(f, 1)] = state


def forward(place, x, operators, block, starting):
    n, _, rows, width = x.shape
    rank = operators[0].shape[1]
    hours, steps = n * rows, 2
    nb = hours // BLK
    halves = jax.ShapeDtypeStruct((2, n // 2, 2, rows, rank), F32)
    halves_spec = pl.BlockSpec((2, n // 2, 1, rows, rank), lambda f, i: (0, 0, f, 0, 0))
    pair, pair_spec = jax.ShapeDtypeStruct((2, rank), F32), pl.BlockSpec((2, rank), lambda f, i: (0, 0))
    op_spec = pl.BlockSpec((width, rank), lambda f, i: (0, 0))
    return pl.pallas_call(
        forward_kernel,
        grid=(2, steps),
        in_specs=[
            pl.BlockSpec(memory_space=pltpu.SMEM),
            pl.BlockSpec((n // steps, 1, rows, width), lambda f, i: (i, f, 0, 0)),
            op_spec,
            op_spec,
            pl.BlockSpec((nb, BLK + 8, BLK + 128), lambda f, i: (f, 0, 0)),
            pl.BlockSpec((2, width), lambda f, i: (0, 0)),
        ],
        out_specs=[halves_spec, pair_spec, pair_spec],
        out_shape=[halves, pair, pair],
        scratch_shapes=[pltpu.VMEM((hours, rank), F32)],
        compiler_params=pltpu.CompilerParams(vmem_limit_bytes=24 * MIB),
        cost_estimate=pl.CostEstimate(
            flops=4 * hours * width * rank, bytes_accessed=4 * hours * width, transcendentals=0
        ),
        name="forward",
    )(place, x, *operators, block, starting)


def backward_kernel(
    f, place_ref, own_ref, other_ref, block_ref, x_ref, enter_ref, keep0_ref, send0_ref, keep1_ref, send1_ref, z_ref, carried, w_ref,
    held, sems,
):
    step = pl.program_id(0)
    rank = own_ref.shape[3]
    quarter = rank // 4

    count, _, _, chunk = held.shape

    def load(i):
        return pltpu.make_async_copy(x_ref.at[:, f, :, pl.ds(i * chunk, chunk)], held.at[i], sems.at[i])

    @pl.when(step == 0)
    def _():
        for i in range(count):
            load(i).start()
        nb = block_ref.shape[0]
        rows = own_ref.shape[2]
        per = BLK // rows
        reverse = jnp.zeros((rank, 1), F32)

        def placed(ref, value, cols, base=0):
            for order in range(2):
                for d in range(4):
                    to = jnp.bitwise_xor(d, place_ref[1])
                    if order == 0:
                        to = jnp.where(to == 0, 0, to % 3 + 1)
                    at = pl.multiple_of(base + to * quarter, quarter)
                    ref[order, pl.ds(at, quarter), cols] = value[d * quarter : (d + 1) * quarter]

        parts = []
        for b in range(nb):
            half, at = divmod(b, nb // 2)
            own = own_ref[at * per : (at + 1) * per, 0].reshape(BLK, rank)
            other = other_ref[at * per : (at + 1) * per, 0].reshape(BLK, rank)
            q = jnp.where(place_ref[0] == half, own.astype(F32), other.astype(F32)).T.astype(BF16)
            high, middle, low = thirds(block_ref[b, :BLK])
            parts.append(
                jnp.dot(
                    jnp.concatenate([q, q, q], axis=1),
                    jnp.concatenate([low, middle, high], axis=0),
                    preferred_element_type=F32,
                )
            )
        for b in reversed(range(nb)):
            out = parts[b] - reverse * block_ref[b, BLK : BLK + 1, :]
            z = out[:, :BLK]
            high = z.astype(BF16)
            cols = slice(b * BLK, (b + 1) * BLK)
            placed(z_ref, high, cols)
            placed(z_ref, (z - high.astype(F32)).astype(BF16), cols, rank)
            reverse = out[:, BLK : BLK + 1]
        placed(carried, jnp.broadcast_to(reverse, carried.shape[1:]), slice(0, carried.shape[2]))

    load(step).wait()
    hours = z_ref.shape[2]
    order = step // (pl.num_programs(0) // 2)
    for t in range(chunk // TILE):
        cols = slice(t * TILE, (t + 1) * TILE)
        w = jnp.dot(z_ref[order], held[step, :, :, cols].reshape(hours, TILE), preferred_element_type=F32)
        w = w[:rank] + w[rank:] - carried[order][:, 0:1] * enter_ref[0, :, cols]
        w_ref[:, cols] = w.astype(BF16)
    for k, (keep_ref, send_ref) in enumerate(((keep0_ref, send0_ref), (keep1_ref, send1_ref))):

        @pl.when(order == k)
        def _():
            keep_ref[...] = w_ref[: rank // 2]
            send_ref[...] = w_ref[rank // 2 :]


def backward(f, place, own, other, block, x, enter):
    n, _, rows, width = x.shape
    hours, rank = n * rows, own.shape[3]
    nb = hours // BLK
    steps = width // NCHUNK // 2
    q_spec = pl.BlockSpec((n // 2, 1, rows, rank), lambda i: (0, 1 - f, 0, 0))
    left = pl.BlockSpec((rank // 2, NCHUNK), lambda i: (0, jnp.minimum(i, steps - 1)))
    right = pl.BlockSpec((rank // 2, NCHUNK), lambda i: (0, jnp.maximum(i - steps, 0)))
    piece = jax.ShapeDtypeStruct((rank // 2, width // 2), BF16)
    return pl.pallas_call(
        functools.partial(backward_kernel, f),
        grid=(2 * steps,),
        in_specs=[
            pl.BlockSpec(memory_space=pltpu.SMEM),
            q_spec,
            q_spec,
            pl.BlockSpec((nb, BLK + 8, BLK + 128), lambda i: (f, 0, 0)),
            pl.BlockSpec(memory_space=pl.ANY),
            pl.BlockSpec((1, 1, NCHUNK), lambda i: (f, 0, i)),
        ],
        out_specs=[left, left, right, right],
        out_shape=[piece] * 4,
        scratch_shapes=[
            pltpu.VMEM((2, 2 * rank, hours), BF16),
            pltpu.VMEM((2, rank, 128), F32),
            pltpu.VMEM((rank, NCHUNK), BF16),
            pltpu.VMEM((2 * steps, n, rows, NCHUNK), BF16),
            pltpu.SemaphoreType.DMA((2 * steps,)),
        ],
        compiler_params=pltpu.CompilerParams(vmem_limit_bytes=51 * MIB),
        cost_estimate=pl.CostEstimate(
            flops=4 * hours * width * rank, bytes_accessed=2 * hours * width, transcendentals=0
        ),
        name="backward",
    )(place, own, other, block, x, enter[:, None])


def cross_kernel(place_ref, own_ref, other_ref, out_ref):
    n, _, rows, rank = own_ref.shape
    out = jnp.zeros(out_ref.shape, F32)
    for ref in (own_ref, other_ref):
        left = ref[:, 0].reshape(n * rows, rank).astype(F32).T.astype(BF16)
        out = out + jnp.dot(left, ref[:, 1].reshape(n * rows, rank), preferred_element_type=F32)
    out_ref[...] = out


def cross(place, own, other):
    rank = own.shape[3]
    whole = pl.BlockSpec(memory_space=pltpu.VMEM)
    return pl.pallas_call(
        cross_kernel,
        out_shape=jax.ShapeDtypeStruct((rank, rank), F32),
        in_specs=[pl.BlockSpec(memory_space=pltpu.SMEM), whole, whole],
        out_specs=whole,
        compiler_params=pltpu.CompilerParams(vmem_limit_bytes=8 * MIB),
        cost_estimate=pl.CostEstimate(flops=2 * own.size * rank, bytes_accessed=4 * own.size, transcendentals=0),
        name="cross",
    )(place, own, other)


def all_to_all(x, axis, groups=None):
    return lax.all_to_all(x, axis, split_axis=0, concat_axis=0, tiled=True, axis_index_groups=groups)


def shifted(x, by):
    n = lax.axis_size("tm")
    return lax.ppermute(x, "tm", [(i, (i + by) % n) for i in range(n)])


def paired(x, by):
    return lax.ppermute(x, "tm", [(i, i ^ by) for i in range(lax.axis_size("tm"))])


def across(x):
    return lax.ppermute(x, "grid", [(g, g ^ 1) for g in range(Y * Z * C)])


def entering(end, gain, start, i):
    message = jnp.concatenate([end, jnp.broadcast_to(gain, end.shape)])
    total, so_far = jnp.zeros_like(end), jnp.ones_like(end)
    for d in range(1, lax.axis_size("tm")):
        got = shifted(message, d)
        total = total + jnp.where(i >= d, so_far * got[:2], 0.0)
        so_far = so_far * jnp.where(i >= d, got[2:4], 1.0)
    return total + so_far * start


def summed_over_hours(pieces):
    keep0, send0, keep1, send1 = pieces
    q = send0.shape[0] // 2
    wide = lambda v: v.astype(F32)
    got0 = paired(send0, 1)
    got1 = paired(send1, 3)
    sent0 = (wide(keep0[q:]) + wide(got0[q:])).astype(BF16)
    sent1 = (wide(keep1[q:]) + wide(got1[:q])).astype(BF16)
    last0, last1 = paired(sent0, 3), paired(sent1, 1)
    left = wide(keep0[:q]) + wide(got0[:q]) + wide(last0)
    right = wide(keep1[:q]) + wide(got1[q:]) + wide(last1)
    return jnp.concatenate([left, right], axis=1), (sent0, sent1)


def per_device(x0, x1, fading, starting, operator0, operator1):
    grid = lax.axis_size("grid")
    rows, _ = x0.shape
    hours = rows * grid
    scale = (hours * lax.axis_size("tm")) ** -0.5
    core, shard = lax.axis_index("grid") & (C - 1), lax.axis_index("tm")
    place = jnp.stack([core, shard]).astype(jnp.int32)
    n = grid // C
    groups = [[k * C + c for k in range(n)] for c in range(C)]
    packed, *tables = prepare(x0, x1, fading, grid)
    rest = (tables, operator0, operator1, place, core, shard, starting)
    packed, rest = lax.optimization_barrier((packed, rest))
    x = all_to_all(packed, "grid")
    x, (tables, *operators, place, core, shard, starting) = lax.optimization_barrier((x, rest))
    block, since, to_end, gain = tables
    (own, other), end, begin = forward(place, x, operators, block, starting)
    enter = entering(end, gain[:, :1], begin, shard)
    enter = enter + across(enter)
    since = lax.dynamic_index_in_dim(since.reshape(2, C, n, rows), core, 1, keepdims=False).transpose(1, 0, 2)
    p = own + across(other) - since[..., None] * enter[None, :, None]
    p, x = lax.optimization_barrier((p.astype(BF16), x))
    p = all_to_all(p, "grid", groups)
    q = p.astype(F32).sum(axis=0).astype(BF16)
    q_own = all_to_all(jnp.broadcast_to(q, p.shape), "grid", groups)
    q_other = across(q_own)
    weight = to_end.reshape(2, grid, rows).transpose(1, 0, 2)[..., None]
    mean = entering((x.astype(F32) * weight).sum(axis=(0, 2)), gain[:, :1], starting, shard)
    w1 = backward(1, place, q_own, q_other, block, x, mean)
    wetness = summed_over_hours(w1)[0] * scale
    w0 = backward(0, place, q_own, q_other, block, x, mean)
    warmth, last = summed_over_hours(w0)
    warmth = warmth * scale
    sent = cross(place, q_own, q_other).reshape(C, -1, q.shape[2])
    sent = lax.dynamic_index_in_dim(sent, core, 0, keepdims=False).astype(BF16)
    got = [shifted(sent, d) for d in range(1, lax.axis_size("tm"))]
    got, _ = lax.optimization_barrier((got, last))
    half = sum((part.astype(F32) for part in got), sent.astype(F32))
    partner = across(half)
    middle = jnp.concatenate([jnp.where(core == 0, half, partner), jnp.where(core == 0, partner, half)])
    return warmth, wetness, middle * scale


def solution(mesh):
    return jax.shard_map(
        per_device,
        mesh=mesh,
        in_specs=(
            P(("tm", "grid"), None),
            P(("tm", "grid"), None),
            P(None, "tm"),
            P(None, "grid"),
            P("grid", None),
            P("grid", None),
        ),
        out_specs=(P("tm", "grid"), P("tm", "grid"), P()),
        check_vma=False,
    )
```

```python
import functools

import jax
import jax.numpy as jnp
from jax import lax
from jax.experimental import pallas as pl
from jax.experimental.pallas import tpu as pltpu
from jax.sharding import PartitionSpec as P


BLK = 256
HALF = BLK // 2
NCHUNK = 768
TILE = 256
Y, Z, C = 4, 4, 2
F32, BF16 = jnp.float32, jnp.bfloat16
HIGHEST = lax.Precision.HIGHEST
MIB = 1 << 20


def thirds(v):
    high = v.astype(BF16)
    v = v - high.astype(F32)
    middle = v.astype(BF16)
    return high, middle, (v - middle.astype(F32)).astype(BF16)


def prepare_kernel(x0_ref, x1_ref, fading_ref, out_ref, block_ref, since_ref, to_end_ref, gain_ref):
    n, _, _, width = out_ref.shape

    nb = fading_ref.shape[1] // BLK
    a = jnp.concatenate([fading_ref[f : f + 1, b * BLK : (b + 1) * BLK] for f in range(2) for b in range(nb)])
    log_a = jnp.log(a)
    r = lax.broadcasted_iota(jnp.int32, (BLK, BLK), 0)
    c = lax.broadcasted_iota(jnp.int32, (BLK, BLK), 1)
    upto = jnp.where(r <= c, 1.0, 0.0)
    r, c = r[:HALF, :HALF], c[:HALF, :HALF]
    inclusive = jnp.dot(log_a, upto, precision=HIGHEST, preferred_element_type=F32)
    exclusive = jnp.where(lax.broadcasted_iota(jnp.int32, a.shape, 1) == 0, 0.0, pltpu.roll(inclusive, 1, 1))
    column = exclusive.T
    fresh = 1.0 - a
    total = inclusive[:, BLK - 1 : BLK]
    for f in range(2):
        sums = [total[f * nb + b : f * nb + b + 1] for b in range(nb)]
        ahead = jnp.zeros_like(sums[0])
        for b in range(nb):
            k = f * nb + b
            row = slice(k, k + 1)
            for i in range(2):
                for j in range(2):
                    down, over = slice(i * HALF, (i + 1) * HALF), slice(j * HALF, (j + 1) * HALF)
                    if i < j:
                        block_ref[k, down, over] = jnp.zeros((HALF, HALF), F32)
                        continue
                    spread = column[down, k : k + 1] - inclusive[row, over]
                    weight = jnp.exp(jnp.minimum(spread, 0.0)) * -fresh[row, over]
                    block_ref[k, down, over] = jnp.where(r == c, 1.0, jnp.where(c < r, weight, 0.0)) if i == j else weight
            block_ref[k, :BLK, BLK:] = jnp.broadcast_to(jnp.exp(column[:, k : k + 1]), (BLK, 128))
            last = jnp.exp(sums[b] - inclusive[row]) * fresh[row]
            block_ref[k, BLK:, :BLK] = jnp.broadcast_to(last, (8, BLK))
            block_ref[k, BLK:, BLK:] = jnp.broadcast_to(-jnp.exp(sums[b]), (8, 128))
            behind = sum(sums[b + 1 :], jnp.zeros_like(ahead))
            since_ref[row] = jnp.exp(ahead + exclusive[row])
            to_end_ref[row] = jnp.exp(behind + (sums[b] - inclusive[row])) * fresh[row]
            ahead = ahead + sums[b]
        gain_ref[f : f + 1] = jnp.broadcast_to(jnp.exp(ahead), (1, BLK))
    for i in range(n):
        for f, x_ref in enumerate((x0_ref, x1_ref)):
            out_ref[i, f] = x_ref[:, i * width : (i + 1) * width]


def prepare(x0, x1, fading, n):
    rows, points = x0.shape
    width = points // n
    count = fading.size // BLK
    whole = pl.BlockSpec(memory_space=pltpu.VMEM)
    return pl.pallas_call(
        prepare_kernel,
        in_specs=[whole, whole, whole],
        out_specs=[whole, whole, whole, whole, whole],
        out_shape=[
            jax.ShapeDtypeStruct((n, 2, rows, width), x0.dtype),
            jax.ShapeDtypeStruct((count, BLK + 8, BLK + 128), F32),
            jax.ShapeDtypeStruct((count, BLK), F32),
            jax.ShapeDtypeStruct((count, BLK), F32),
            jax.ShapeDtypeStruct((2, BLK), F32),
        ],
        compiler_params=pltpu.CompilerParams(vmem_limit_bytes=20 * MIB),
        cost_estimate=pl.CostEstimate(flops=0, bytes_accessed=8 * x0.size, transcendentals=0),
        name="prepare",
    )(x0, x1, fading)


def exact_dot(left, right):
    lh, lm, ll = thirds(left)
    rh, rm, rl = thirds(right)
    return jnp.dot(
        jnp.concatenate([ll, lm, lh, lm, lh, lh], axis=1),
        jnp.concatenate([rh, rm, rl, rh, rm, rh], axis=0),
        preferred_element_type=F32,
    )


def forward_kernel(
    place_ref, x_ref, op0_ref, op1_ref, block_ref, start_ref, p_ref, end_ref, begin_ref, y_ref
):
    f, step = pl.program_id(0), pl.program_id(1)
    count, _, rows, width = x_ref.shape
    hours, rank = y_ref.shape
    nb = hours // BLK
    at = pl.multiple_of(step * (count * rows), count * rows)

    def products(k, op_ref):
        y_ref[pl.ds(at, count * rows)] = jnp.dot(
            x_ref[:, 0].reshape(count * rows, width), op_ref[...], preferred_element_type=F32
        )

        @pl.when(step == 0)
        def _():
            parts = thirds(start_ref[k : k + 1])
            start = jnp.concatenate([part.astype(F32) for part in parts] + [jnp.zeros((5, width), F32)])
            begin = jnp.dot(start.astype(BF16), op_ref[...], preferred_element_type=F32)
            begin_ref[k : k + 1] = begin[0:1] + begin[1:2] + begin[2:3]

    for k, op_ref in enumerate((op0_ref, op1_ref)):

        @pl.when(f == k)
        def _():
            products(k, op_ref)

    @pl.when(step == pl.num_programs(1) - 1)
    def _():
        state = jnp.zeros((1, rank), F32)
        per = BLK // rows
        outs = [exact_dot(block_ref[b, :, :BLK], y_ref[b * BLK : (b + 1) * BLK]) for b in range(nb)]
        for b, out in enumerate(outs):
            out = out - block_ref[b, :, BLK : BLK + 1] * state
            half, at = divmod(b, nb // 2)
            slot = jnp.bitwise_xor(half, place_ref[0])
            p_ref[slot, at * per : (at + 1) * per, 0] = out[:BLK].reshape(per, rows, rank)
            state = out[BLK : BLK + 1]
        end_ref[pl.ds(f, 1)] = state


def forward(place, x, operators, block, starting):
    n, _, rows, width = x.shape
    rank = operators[0].shape[1]
    hours, steps = n * rows, 2
    nb = hours // BLK
    halves = jax.ShapeDtypeStruct((2, n // 2, 2, rows, rank), F32)
    halves_spec = pl.BlockSpec((2, n // 2, 1, rows, rank), lambda f, i: (0, 0, f, 0, 0))
    pair, pair_spec = jax.ShapeDtypeStruct((2, rank), F32), pl.BlockSpec((2, rank), lambda f, i: (0, 0))
    op_spec = pl.BlockSpec((width, rank), lambda f, i: (0, 0))
    return pl.pallas_call(
        forward_kernel,
        grid=(2, steps),
        in_specs=[
            pl.BlockSpec(memory_space=pltpu.SMEM),
            pl.BlockSpec((n // steps, 1, rows, width), lambda f, i: (i, f, 0, 0)),
            op_spec,
            op_spec,
            pl.BlockSpec((nb, BLK + 8, BLK + 128), lambda f, i: (f, 0, 0)),
            pl.BlockSpec((2, width), lambda f, i: (0, 0)),
        ],
        out_specs=[halves_spec, pair_spec, pair_spec],
        out_shape=[halves, pair, pair],
        scratch_shapes=[pltpu.VMEM((hours, rank), F32)],
        compiler_params=pltpu.CompilerParams(vmem_limit_bytes=24 * MIB),
        cost_estimate=pl.CostEstimate(
            flops=4 * hours * width * rank, bytes_accessed=4 * hours * width, transcendentals=0
        ),
        name="forward",
    )(place, x, *operators, block, starting)


def backward_kernel(
    f, place_ref, own_ref, other_ref, block_ref, x_ref, enter_ref, keep0_ref, send0_ref, keep1_ref, send1_ref, z_ref, carried, w_ref,
    held, sems,
):
    step = pl.program_id(0)
    rank = own_ref.shape[3]
    quarter = rank // 4

    count, _, _, chunk = held.shape

    def load(i):
        return pltpu.make_async_copy(x_ref.at[:, f, :, pl.ds(i * chunk, chunk)], held.at[i], sems.at[i])

    @pl.when(step == 0)
    def _():
        for i in range(count):
            load(i).start()
        nb = block_ref.shape[0]
        rows = own_ref.shape[2]
        per = BLK // rows
        reverse = jnp.zeros((rank, 1), F32)

        def placed(ref, value, cols, base=0):
            for order in range(2):
                for d in range(4):
                    to = jnp.bitwise_xor(d, place_ref[1])
                    if order == 0:
                        to = jnp.where(to == 0, 0, to % 3 + 1)
                    at = pl.multiple_of(base + to * quarter, quarter)
                    ref[order, pl.ds(at, quarter), cols] = value[d * quarter : (d + 1) * quarter]

        parts = []
        for b in range(nb):
            half, at = divmod(b, nb // 2)
            own = own_ref[at * per : (at + 1) * per, 0].reshape(BLK, rank)
            other = other_ref[at * per : (at + 1) * per, 0].reshape(BLK, rank)
            q = jnp.where(place_ref[0] == half, own.astype(F32), other.astype(F32)).T.astype(BF16)
            high, middle, low = thirds(block_ref[b, :BLK])
            parts.append(
                jnp.dot(
                    jnp.concatenate([q, q, q], axis=1),
                    jnp.concatenate([low, middle, high], axis=0),
                    preferred_element_type=F32,
                )
            )
        for b in reversed(range(nb)):
            out = parts[b] - reverse * block_ref[b, BLK : BLK + 1, :]
            z = out[:, :BLK]
            high = z.astype(BF16)
            cols = slice(b * BLK, (b + 1) * BLK)
            placed(z_ref, high, cols)
            placed(z_ref, (z - high.astype(F32)).astype(BF16), cols, rank)
            reverse = out[:, BLK : BLK + 1]
        placed(carried, jnp.broadcast_to(reverse, carried.shape[1:]), slice(0, carried.shape[2]))

    load(step).wait()
    hours = z_ref.shape[2]
    order = step // (pl.num_programs(0) // 2)
    for t in range(chunk // TILE):
        cols = slice(t * TILE, (t + 1) * TILE)
        w = jnp.dot(z_ref[order], held[step, :, :, cols].reshape(hours, TILE), preferred_element_type=F32)
        w = w[:rank] + w[rank:] - carried[order][:, 0:1] * enter_ref[0, :, cols]
        w_ref[:, cols] = w.astype(BF16)
    for k, (keep_ref, send_ref) in enumerate(((keep0_ref, send0_ref), (keep1_ref, send1_ref))):

        @pl.when(order == k)
        def _():
            keep_ref[...] = w_ref[: rank // 2]
            send_ref[...] = w_ref[rank // 2 :]


def backward(f, place, own, other, block, x, enter):
    n, _, rows, width = x.shape
    hours, rank = n * rows, own.shape[3]
    nb = hours // BLK
    steps = width // NCHUNK // 2
    q_spec = pl.BlockSpec((n // 2, 1, rows, rank), lambda i: (0, 1 - f, 0, 0))
    left = pl.BlockSpec((rank // 2, NCHUNK), lambda i: (0, jnp.minimum(i, steps - 1)))
    right = pl.BlockSpec((rank // 2, NCHUNK), lambda i: (0, jnp.maximum(i - steps, 0)))
    piece = jax.ShapeDtypeStruct((rank // 2, width // 2), BF16)
    return pl.pallas_call(
        functools.partial(backward_kernel, f),
        grid=(2 * steps,),
        in_specs=[
            pl.BlockSpec(memory_space=pltpu.SMEM),
            q_spec,
            q_spec,
            pl.BlockSpec((nb, BLK + 8, BLK + 128), lambda i: (f, 0, 0)),
            pl.BlockSpec(memory_space=pl.ANY),
            pl.BlockSpec((1, 1, NCHUNK), lambda i: (f, 0, i)),
        ],
        out_specs=[left, left, right, right],
        out_shape=[piece] * 4,
        scratch_shapes=[
            pltpu.VMEM((2, 2 * rank, hours), BF16),
            pltpu.VMEM((2, rank, 128), F32),
            pltpu.VMEM((rank, NCHUNK), BF16),
            pltpu.VMEM((2 * steps, n, rows, NCHUNK), BF16),
            pltpu.SemaphoreType.DMA((2 * steps,)),
        ],
        compiler_params=pltpu.CompilerParams(vmem_limit_bytes=51 * MIB),
        cost_estimate=pl.CostEstimate(
            flops=4 * hours * width * rank, bytes_accessed=2 * hours * width, transcendentals=0
        ),
        name="backward",
    )(place, own, other, block, x, enter[:, None])


def cross_kernel(place_ref, own_ref, other_ref, out_ref):
    n, _, rows, rank = own_ref.shape
    out = jnp.zeros(out_ref.shape, F32)
    for ref in (own_ref, other_ref):
        left = ref[:, 0].reshape(n * rows, rank).astype(F32).T.astype(BF16)
        out = out + jnp.dot(left, ref[:, 1].reshape(n * rows, rank), preferred_element_type=F32)
    out_ref[...] = out


def cross(place, own, other):
    rank = own.shape[3]
    whole = pl.BlockSpec(memory_space=pltpu.VMEM)
    return pl.pallas_call(
        cross_kernel,
        out_shape=jax.ShapeDtypeStruct((rank, rank), F32),
        in_specs=[pl.BlockSpec(memory_space=pltpu.SMEM), whole, whole],
        out_specs=whole,
        compiler_params=pltpu.CompilerParams(vmem_limit_bytes=8 * MIB),
        cost_estimate=pl.CostEstimate(flops=2 * own.size * rank, bytes_accessed=4 * own.size, transcendentals=0),
        name="cross",
    )(place, own, other)


def all_to_all(x, axis, groups=None):
    return lax.all_to_all(x, axis, split_axis=0, concat_axis=0, tiled=True, axis_index_groups=groups)


def shifted(x, by):
    n = lax.axis_size("tm")
    return lax.ppermute(x, "tm", [(i, (i + by) % n) for i in range(n)])


def paired(x, by):
    return lax.ppermute(x, "tm", [(i, i ^ by) for i in range(lax.axis_size("tm"))])


def across(x):
    return lax.ppermute(x, "grid", [(g, g ^ 1) for g in range(Y * Z * C)])


def entering(end, gain, start, i):
    message = jnp.concatenate([end, jnp.broadcast_to(gain, end.shape)])
    total, so_far = jnp.zeros_like(end), jnp.ones_like(end)
    for d in range(1, lax.axis_size("tm")):
        got = shifted(message, d)
        total = total + jnp.where(i >= d, so_far * got[:2], 0.0)
        so_far = so_far * jnp.where(i >= d, got[2:4], 1.0)
    return total + so_far * start


def summed_over_hours(pieces):
    keep0, send0, keep1, send1 = pieces
    q = send0.shape[0] // 2
    wide = lambda v: v.astype(F32)
    got0 = paired(send0, 1)
    got1 = paired(send1, 3)
    sent0 = (wide(keep0[q:]) + wide(got0[q:])).astype(BF16)
    sent1 = (wide(keep1[q:]) + wide(got1[:q])).astype(BF16)
    last0, last1 = paired(sent0, 3), paired(sent1, 1)
    left = wide(keep0[:q]) + wide(got0[:q]) + wide(last0)
    right = wide(keep1[:q]) + wide(got1[q:]) + wide(last1)
    return jnp.concatenate([left, right], axis=1), (sent0, sent1)


def per_device(x0, x1, fading, starting, operator0, operator1):
    grid = lax.axis_size("grid")
    rows, _ = x0.shape
    hours = rows * grid
    scale = (hours * lax.axis_size("tm")) ** -0.5
    core, shard = lax.axis_index("grid") & (C - 1), lax.axis_index("tm")
    place = jnp.stack([core, shard]).astype(jnp.int32)
    n = grid // C
    groups = [[k * C + c for k in range(n)] for c in range(C)]
    packed, *tables = prepare(x0, x1, fading, grid)
    rest = (tables, operator0, operator1, place, core, shard, starting)
    packed, rest = lax.optimization_barrier((packed, rest))
    x = all_to_all(packed, "grid")
    x, (tables, *operators, place, core, shard, starting) = lax.optimization_barrier((x, rest))
    block, since, to_end, gain = tables
    (own, other), end, begin = forward(place, x, operators, block, starting)
    enter = entering(end, gain[:, :1], begin, shard)
    enter = enter + across(enter)
    since = lax.dynamic_index_in_dim(since.reshape(2, C, n, rows), core, 1, keepdims=False).transpose(1, 0, 2)
    p = own + across(other) - since[..., None] * enter[None, :, None]
    p, x = lax.optimization_barrier((p.astype(BF16), x))
    p = all_to_all(p, "grid", groups)
    q = p.astype(F32).sum(axis=0).astype(BF16)
    q_own = all_to_all(jnp.broadcast_to(q, p.shape), "grid", groups)
    q_other = across(q_own)
    weight = to_end.reshape(2, grid, rows).transpose(1, 0, 2)[..., None]
    mean = entering((x.astype(F32) * weight).sum(axis=(0, 2)), gain[:, :1], starting, shard)
    w1 = backward(1, place, q_own, q_other, block, x, mean)
    wetness = summed_over_hours(w1)[0] * scale
    w0 = backward(0, place, q_own, q_other, block, x, mean)
    warmth, last = summed_over_hours(w0)
    warmth = warmth * scale
    sent = cross(place, q_own, q_other).reshape(C, -1, q.shape[2])
    sent = lax.dynamic_index_in_dim(sent, core, 0, keepdims=False).astype(BF16)
    got = [shifted(sent, d) for d in range(1, lax.axis_size("tm"))]
    got, _ = lax.optimization_barrier((got, last))
    half = sum((part.astype(F32) for part in got), sent.astype(F32))
    partner = across(half)
    middle = jnp.concatenate([jnp.where(core == 0, half, partner), jnp.where(core == 0, partner, half)])
    return warmth, wetness, middle * scale


def solution(mesh):
    return jax.shard_map(
        per_device,
        mesh=mesh,
        in_specs=(
            P(("tm", "grid"), None),
            P(("tm", "grid"), None),
            P(None, "tm"),
            P(None, "grid"),
            P("grid", None),
            P("grid", None),
        ),
        out_specs=(P("tm", "grid"), P("tm", "grid"), P()),
        check_vma=False,
    )
```
